256 devices in a mesh: tm: 16 (over x, z_lo, core), tp: 16 (over y, z_hi).
Axes of the slice: x: 4, y: 4, z: 8 (z_hi: 4, z_lo: 2; z = z_hi * 2 + z_lo), core: 2. Of those that a mesh axis runs over, the one named last changes fastest.
Arguments:
- states: float32 [4096, 6144], P(('tm', 'tp')), may hold values from -6 to 6
- norm_gain: float32 [6144], replicated, may hold values from 0.5 to 1.5
- qkv_weight: bfloat16 [6144, 3, 4096], P(None, None, 'tp'), may hold values from -1 to 1
- qk_gain: float32 [2, 4096], P(None, 'tp'), may hold values from 1.2 to 5.5
- out_weight: bfloat16 [4096, 6144], P('tp'), may hold values from -0.09375 to 0.09375
- segment_lengths: int32 [16], replicated, may hold values from 1 to 256, 3072 in all
Outputs:
- denoised: float32 [4096, 6144], P(('tm', 'tp'))
The draws below stay inside these ranges and needn't reach their ends.
Inputs may be any that keep to these rules, and one draw needn't show every extreme that they name: `segment_lengths`: the lengths sum to 3072 and one segment is full.
All inputs are finite; a program needn't handle non-finite values.
Results may differ from the reference program's by a relative error of at most 0.015.
Values may be sent and summed in bfloat16 or wider, within the bound.
No kernel may reach another device: no remote copies, remote signals or barrier semaphores. Data moves between devices by JAX's collectives and lax.ppermute only.
A program may use at most 128 MiB of HBM per device.

```python
import math
import jax
import jax.numpy as jnp
import numpy as np
from jax import lax

D = 6144
HEADS = 32
HD = 128
SEG = 256
STEPS = 2
TOKENS = 4096
N_TM = 16
N_TP = 16


def draw_qkv_weight(key, part):
    limit = math.sqrt(3.0 / D)
    first = jax.random.uniform(jax.random.fold_in(key, 11), (D, HEADS * HD), jnp.float32, -limit, limit)
    second = jax.random.uniform(jax.random.fold_in(key, 12), (D, HEADS * HD), jnp.float32, -limit, limit)
    third = jax.random.uniform(jax.random.fold_in(key, 13), (D, HEADS * HD), jnp.float32, -limit, limit)
    stacked = jnp.stack([first, second, third], axis=1)
    return stacked.astype(jnp.bfloat16)


def draw_qk_gain(key, part):
    gains = jnp.exp(jax.random.uniform(jax.random.fold_in(key, 23), (2, HEADS * HD), jnp.float32, math.log(1.2), math.log(2.2)))
    return gains


def steps_of(rng, shape, split, smallest, top_value):
    loudness, own = 1.0, jax.random.fold_in(rng, 6)
    for axis_at, blocks in split:
        heights = jnp.exp(jax.random.uniform(jax.random.fold_in(own, axis_at), (blocks,), jnp.float32, smallest / len(split), top_value / len(split)))
        loudness = loudness * jnp.repeat(heights, shape[axis_at] // blocks).reshape([-1 if axis == axis_at else 1 for axis in range(len(shape))])
    return loudness


def profile(number_of, total, most, slope):
    loads = [(1 << 20) // math.isqrt(standing ** slope) + 1 for standing in range(2, number_of + 1)]
    rest, given = total - most - (number_of - 1), [1] * (number_of - 1)
    while rest > 0:
        free = [i for i in range(number_of - 1) if given[i] < most]
        pool, left = sum([loads[i] for i in free]), rest
        for i in free:
            extra = min(most - given[i], max(1, left * loads[i] // pool), rest)
            given[i] = given[i] + extra
            rest = rest - extra
    return np.array([most] + given)


def uneven(key, count, total, reach, skew):
    if count == 2:
        one = jax.random.randint(key, (), max(1, total - reach), min(reach, total - 1) + 1)
        return jnp.stack([one, total - one])
    tallies = jnp.asarray(profile(count, total, reach, skew), jnp.int32)
    pairs = (count - 1) // 2
    giver, sink = tallies[1:1 + 2 * pairs:2], tallies[2:2 + 2 * pairs:2]
    slack = jnp.minimum(giver - 1, reach - sink)
    passed = jax.random.randint(jax.random.fold_in(key, 1), (pairs,), 0, 1 << 20) % (slack + 1)
    tallies = tallies.at[1:1 + 2 * pairs:2].set(giver - passed).at[2:2 + 2 * pairs:2].set(sink + passed)
    return tallies[jax.random.permutation(jax.random.fold_in(key, 2), count)]


def centred(stream_key, extent, scale, bound, pieces=(), held_as=jnp.bfloat16):
    loudness = steps_of(stream_key, extent, pieces, -0.22, 0.18) if pieces else 1.0
    result = jax.random.normal(stream_key, extent, jnp.float32) * scale * loudness
    return jnp.minimum(jnp.maximum(result, -bound), bound).astype(held_as)


def setup_inputs(seed: int = 0) -> dict:
    seeds = jax.random.split(jax.random.key(seed), 7)
    return {
        "states": centred(seeds[0], (TOKENS, D), 1.0, 6.0, ((0, 256),), jnp.float32),
        "norm_gain": jnp.clip(1.0 + 0.1 * jax.random.normal(seeds[1], (D,), jnp.float32), 0.5, 1.5),
        "qkv_weight": draw_qkv_weight(jax.random.fold_in(seeds[6], 71), 0),
        "qk_gain": draw_qk_gain(jax.random.fold_in(seeds[6], 71), 0),
        "out_weight": centred(seeds[4], (HEADS * HD, D), (HEADS * HD) ** -0.5, 0.09375, ((0, 16),)),
        "segment_lengths": uneven(seeds[5], N_TM, 3 * N_TM * SEG // 4, SEG, 1).astype(jnp.int32),
    }


eps_norm = 1e-06
step_size = -0.5

def rms_scale(values, gain):
    mean_square = lax.optimization_barrier(jnp.mean(values * values, axis=-1, keepdims=True))
    return values * lax.rsqrt(mean_square + eps_norm) * gain

def reference(states, norm_gain, qkv_weight, qk_gain, out_weight, segment_lengths):
    inner = HEADS * HD
    group_cols = inner // N_TP
    wmat = qkv_weight.reshape(D, 3 * inner)
    q_gain = qk_gain[0].reshape(HEADS, HD)
    k_gain = qk_gain[1].reshape(HEADS, HD)
    out_groups = out_weight.reshape(N_TP, group_cols, D).astype(jnp.float32)
    key_index = jnp.arange(TOKENS, dtype=jnp.int32)
    key_seg = key_index // SEG
    key_pos = key_index - key_seg * SEG
    key_len = segment_lengths[key_seg]
    current = states
    for step_index in range(STEPS):
        normed = rms_scale(current, norm_gain).astype(jnp.bfloat16)
        qkv = jnp.dot(normed, wmat, preferred_element_type=jnp.float32)
        queries = rms_scale(qkv[:, :inner].reshape(TOKENS, HEADS, HD), q_gain).astype(jnp.bfloat16)
        keys = rms_scale(qkv[:, inner:2 * inner].reshape(TOKENS, HEADS, HD), k_gain).astype(jnp.bfloat16)
        values = qkv[:, 2 * inner:].reshape(TOKENS, HEADS, HD).astype(jnp.bfloat16)
        keys_wide = keys.astype(jnp.float32)
        values_wide = values.astype(jnp.float32)

        def one_segment(seg_index):
            query_rows = lax.dynamic_slice_in_dim(queries, (seg_index * SEG).astype(jnp.int32), SEG, 0).astype(jnp.float32)
            scores = jnp.einsum('qhd,khd->hqk', query_rows, keys_wide) * HD ** (-0.5)
            valid = (key_seg <= seg_index) & (key_pos < key_len)
            masked = jnp.where(valid[None, None, :], scores, -1e+30)
            row_max = lax.optimization_barrier(jnp.max(masked, axis=-1, keepdims=True))
            expo = jnp.where(valid[None, None, :], jnp.exp(masked - row_max), 0.0)
            denom = lax.optimization_barrier(jnp.sum(expo, axis=-1))
            weights = expo.astype(jnp.bfloat16).astype(jnp.float32)
            summed = jnp.einsum('hqk,khd->qhd', weights, values_wide)
            attended = (summed / jnp.transpose(denom)[:, :, None]).astype(jnp.bfloat16)
            grouped = attended.reshape(SEG, N_TP, group_cols).astype(jnp.float32)
            partial_terms = jnp.einsum('sgk,gkd->gsd', grouped, out_groups)
            partial_terms = partial_terms.astype(jnp.bfloat16).astype(jnp.float32)
            return lax.optimization_barrier(jnp.sum(partial_terms, axis=0))
        velocity = lax.map(one_segment, jnp.arange(N_TM, dtype=jnp.int32)).reshape(TOKENS, D)
        current = current + step_size * velocity
    return current
```

```python
import jax
import jax.numpy as jnp
from jax import lax
from jax.experimental import pallas as pl
from jax.experimental.pallas import tpu as pltpu
from jax.sharding import Mesh, PartitionSpec as P

HD = 128
STEPS = 2
SEG = 256
ROWS = 16
eps_norm = 1e-06
step_size = -0.5
f32 = jnp.float32
bf16 = jnp.bfloat16
SCORE_SCALE = 1.4426950408889634 * HD ** (-0.5)


def pp(value, axis, steps):
    count = lax.axis_size(axis)
    return lax.ppermute(value, axis, [(i, (i + steps) % count) for i in range(count)])


def ring_gather(a, b, axis):
    a_m1 = pp(a, axis, 1)
    b_p1 = pp(b, axis, -1)
    b_m1 = pp(b, axis, 1)
    a_p1 = pp(a, axis, -1)
    a_m2 = pp(a_m1, axis, 1)
    b_p2 = pp(b_p1, axis, -1)
    return (a, b, a_p1, b_p1), (a_m2, b_p2, a_m1, b_m1)


def gather_tp(a, b):
    first, second = ring_gather(a, b, "zh")
    first, second = ring_gather(jnp.concatenate(first, 0), jnp.concatenate(second, 0), "y")
    return jnp.concatenate(first + second, 0)


def add(one, other):
    return (one.astype(f32) + other.astype(f32)).astype(bf16)


def ring_scatter(p0, p1a, p1b, p2a, p2b, p3a, p3b, axis):
    ra = pp(p2a, axis, 1)
    rb = pp(p2b, axis, -1)
    t1 = pp(p1b, axis, 1)
    t3 = pp(p3a, axis, -1)
    s1 = pp(add(p1a, ra), axis, 1)
    s3 = pp(add(p3b, rb), axis, -1)
    h = s1.shape[0]
    upper = p0[:h].astype(f32) + s1.astype(f32) + t3.astype(f32)
    lower = p0[h:].astype(f32) + t1.astype(f32) + s3.astype(f32)
    return upper, lower


def scatter_tp(mid, out):
    upper, lower = ring_scatter(
        out[:64], out[64:96], mid[:32], mid[32:64], mid[64:96], mid[96:], out[96:], "y"
    )
    upper = upper.astype(bf16)
    lower = lower.astype(bf16)
    return ring_scatter(
        upper[:16], upper[16:24], upper[24:], lower[:8], lower[8:16], lower[16:24], lower[24:], "zh"
    )


def exchange_kv(kv):
    other = pp(kv, "zl", 1)
    own_m1 = pp(kv, "x", 1)
    own_p1 = pp(kv, "x", -1)
    other_p1 = pp(other, "x", -1)
    other_m1 = pp(other, "x", 1)
    own_m2 = pp(own_m1, "x", 1)
    other_p2 = pp(other_p1, "x", -1)
    here = [kv, other, own_m1, other_m1, own_p1, other_p1, own_m2, other_p2]
    return here + [pp(piece, "c", 1) for piece in here]


def piece_segments():
    where = [(0, 0), (0, 1), (3, 0), (3, 1), (1, 0), (1, 1), (2, 0), (2, 1)]
    x, zl, c = (lax.axis_index(name) for name in ("x", "zl", "c"))
    ids = []
    for dc in range(2):
        for dx, dz in where:
            ids.append(((x + dx) % 4) * 4 + ((zl + dz) % 2) * 2 + (c + dc) % 2)
    return jnp.stack(ids).astype(jnp.int32)


def qkv_body(h_ref, w_ref, gain_ref, q_ref, kv_ref, acc):
    step = pl.program_id(0)
    h = h_ref[...]
    for part in range(3):
        product = jnp.dot(h, w_ref[part], preferred_element_type=f32)

        @pl.when(step == 0)
        def _():
            acc[part] = product

        @pl.when(step > 0)
        def _():
            acc[part] += product

    @pl.when(step == pl.num_programs(0) - 1)
    def _():
        for head in range(2):
            cols = pl.ds(head * HD, HD)
            for part in range(2):
                value = acc[part, :, cols]
                scale = lax.rsqrt(jnp.mean(value * value, axis=-1, keepdims=True) + eps_norm)
                value = (value * scale * gain_ref[part : part + 1, cols]).astype(bf16)
                if part == 0:
                    q_ref[:, cols] = value
                else:
                    kv_ref[:, cols] = value
        kv_ref[:, pl.ds(2 * HD, 2 * HD)] = acc[2].astype(bf16)


def qkv_call(h, w, gain):
    width = h.shape[1]
    block = 1024
    return pl.pallas_call(
        qkv_body,
        grid=(width // block,),
        in_specs=[
            pl.BlockSpec((SEG, block), lambda k: (0, k)),
            pl.BlockSpec((3, block, 2 * HD), lambda k: (0, k, 0)),
            pl.BlockSpec((2, 2 * HD), lambda k: (0, 0)),
        ],
        out_specs=[
            pl.BlockSpec((SEG, 2 * HD), lambda k: (0, 0)),
            pl.BlockSpec((SEG, 4 * HD), lambda k: (0, 0)),
        ],
        out_shape=[
            jax.ShapeDtypeStruct((SEG, 2 * HD), bf16),
            jax.ShapeDtypeStruct((SEG, 4 * HD), bf16),
        ],
        scratch_shapes=[pltpu.VMEM((3, SEG, 2 * HD), f32)],
        name="qkv",
    )(h, w, gain)


def attend_body(ids_ref, len_ref, pos_ref, q_ref, *rest):
    pieces = rest[:16]
    mid_ref, out_ref, held, top, acc, arrived = rest[16:]
    copies = [
        pltpu.make_async_copy(piece, held.at[number], arrived.at[number])
        for number, piece in enumerate(pieces)
    ]
    for copy in copies:
        copy.start()
    own = ids_ref[0]
    pos = pos_ref[...]
    ones = jnp.ones((SEG, HD), bf16)
    top[...] = jnp.full(top.shape, -1e30, f32)
    acc[...] = jnp.zeros(acc.shape, f32)

    @pl.loop(0, 16)
    def _(number):
        pltpu.make_async_copy(pieces[0], held.at[number], arrived.at[number]).wait()

        @pl.when(ids_ref[number] <= own)
        def _():
            valid = pos < len_ref[ids_ref[number]]
            for head in range(2):
                cols = pl.ds(head * HD, HD)
                scores = lax.dot_general(
                    q_ref[:, cols],
                    held[number, :, cols],
                    (((1,), (1,)), ((), ())),
                    preferred_element_type=f32,
                )
                scores = jnp.where(valid, scores * SCORE_SCALE, -1e30)
                before = top[head][:, :1]
                best = jnp.maximum(jnp.max(scores, axis=-1, keepdims=True), before)
                factor = jnp.exp2(before - best)
                weights = jnp.exp2(scores - best).astype(bf16)
                values = held[number, :, pl.ds((2 + head) * HD, HD)]
                extended = jnp.concatenate([values, ones], axis=1)
                update = jnp.dot(weights, extended, preferred_element_type=f32)
                acc[head] = acc[head] * factor + update
                top[head] = jnp.broadcast_to(best, (SEG, HD))

    for head in range(2):
        cols = pl.ds(head * HD, HD)
        attended = (acc[head, :, :HD] / acc[head, :, HD:]).astype(bf16)
        mid_ref[:, cols] = attended[96:224]
        out_ref[:96, cols] = attended[:96]
        out_ref[96:, cols] = attended[224:]


def attend_call(ids, lengths, pos, q, pieces):
    vmem = pl.BlockSpec(memory_space=pltpu.VMEM)
    smem = pl.BlockSpec(memory_space=pltpu.SMEM)
    anywhere = pl.BlockSpec(memory_space=pl.ANY)
    half = jax.ShapeDtypeStruct((SEG // 2, 2 * HD), bf16)
    return pl.pallas_call(
        attend_body,
        in_specs=[smem, smem, vmem, vmem] + [anywhere] * 16,
        out_specs=[vmem, vmem],
        out_shape=[half, half],
        scratch_shapes=[
            pltpu.VMEM((16, SEG, 4 * HD), bf16),
            pltpu.VMEM((2, SEG, HD), f32),
            pltpu.VMEM((2, SEG, 2 * HD), f32),
            pltpu.SemaphoreType.DMA((16,)),
        ],
        name="attend",
    )(ids, lengths, pos, q, *pieces)


def project_body(a_ref, w_ref, o_ref):
    o_ref[...] = jnp.dot(a_ref[...], w_ref[...], preferred_element_type=f32).astype(bf16)


def project_call(attended, w):
    rows, inner = attended.shape
    width = w.shape[1]
    block = 1536
    return pl.pallas_call(
        project_body,
        grid=(width // block,),
        in_specs=[
            pl.BlockSpec((rows, inner), lambda k: (0, 0)),
            pl.BlockSpec((inner, block), lambda k: (0, k)),
        ],
        out_specs=pl.BlockSpec((rows, block), lambda k: (0, k)),
        out_shape=jax.ShapeDtypeStruct((rows, width), bf16),
        name="project",
    )(attended, w)


def normed(current, gain):
    mean_square = jnp.mean(current * current, axis=-1, keepdims=True)
    return (current * lax.rsqrt(mean_square + eps_norm) * gain).astype(bf16)


def shards(states, norm_gain, qkv_weight, qk_gain, out_weight, segment_lengths):
    w = jnp.transpose(qkv_weight, (1, 0, 2))
    y, zh = lax.axis_index("y"), lax.axis_index("zh")
    row = jnp.arange(SEG, dtype=jnp.int32)
    device = (y + row // 64) % 4 * 4 + (zh + row // 16 % 4) % 4
    pos = (device * ROWS + row % ROWS)[None, :]
    ids = piece_segments()

    def one_step(step_index, current):
        h = normed(current, norm_gain)
        gathered = gather_tp(h[: ROWS // 2], h[ROWS // 2 :])
        q, kv = qkv_call(gathered, w, qk_gain)
        mid, out = attend_call(ids, segment_lengths, pos, q, exchange_kv(kv))
        upper, lower = scatter_tp(project_call(mid, out_weight), project_call(out, out_weight))
        return current + step_size * jnp.concatenate([upper, lower], 0)

    return lax.fori_loop(0, STEPS, one_step, states)


def solution(mesh):
    inner = Mesh(mesh.devices.reshape(4, 2, 2, 4, 4), ("x", "zl", "c", "y", "zh"))
    tm, tp = ("x", "zl", "c"), ("y", "zh")
    return jax.shard_map(
        shards,
        mesh=inner,
        in_specs=(P(tm + tp, None), P(), P(None, None, tp), P(None, tp), P(tp, None), P()),
        out_specs=P(tm + tp, None),
        check_vma=False,
    )
```

```python
import jax
import jax.numpy as jnp
from jax import lax
from jax.experimental import pallas as pl
from jax.experimental.pallas import tpu as pltpu
from jax.sharding import Mesh, PartitionSpec as P

HD = 128
STEPS = 2
SEG = 256
ROWS = 16
eps_norm = 1e-06
step_size = -0.5
f32 = jnp.float32
bf16 = jnp.bfloat16
SCORE_SCALE = 1.4426950408889634 * HD ** (-0.5)


def pp(value, axis, steps):
    count = lax.axis_size(axis)
    return lax.ppermute(value, axis, [(i, (i + steps) % count) for i in range(count)])


def ring_gather(a, b, axis):
    a_m1 = pp(a, axis, 1)
    b_p1 = pp(b, axis, -1)
    b_m1 = pp(b, axis, 1)
    a_p1 = pp(a, axis, -1)
    a_m2 = pp(a_m1, axis, 1)
    b_p2 = pp(b_p1, axis, -1)
    return (a, b, a_p1, b_p1), (a_m2, b_p2, a_m1, b_m1)


def gather_tp(a, b):
    first, second = ring_gather(a, b, "zh")
    first, second = ring_gather(jnp.concatenate(first, 0), jnp.concatenate(second, 0), "y")
    return first + second


def held(*arrays):
    return [pltpu.with_memory_space_constraint(value, pltpu.VMEM) for value in arrays]


def local_call(body, name, out, *operands, scratch=()):
    vmem = pl.BlockSpec(memory_space=pltpu.VMEM)
    smem = pl.BlockSpec(memory_space=pltpu.SMEM)
    small = [value.ndim == 1 for value in operands]
    return pl.pallas_call(
        body,
        in_specs=[smem if is_small else vmem for is_small in small],
        out_specs=[vmem] * len(out),
        out_shape=[pltpu.VMEM(shape, dtype) for shape, dtype in out],
        scratch_shapes=scratch,
        compiler_params=pltpu.CompilerParams(vmem_limit_bytes=24 << 20),
        name=name,
    )(*[value if is_small else held(value)[0] for value, is_small in zip(operands, small)])


def prefetch(source, after, part=None):
    def body(after_ref, source_ref, out_ref, arrived):
        del after_ref
        taken = source_ref if part is None else source_ref.at[part]
        copy = pltpu.make_async_copy(taken, out_ref, arrived)
        copy.start()
        copy.wait()

    shape = source.shape if part is None else source.shape[1:]
    anywhere = pl.BlockSpec(memory_space=pl.ANY)
    return pl.pallas_call(
        body,
        in_specs=[anywhere, anywhere],
        out_specs=pl.BlockSpec(memory_space=pltpu.VMEM),
        out_shape=pltpu.VMEM(shape, source.dtype),
        scratch_shapes=[pltpu.SemaphoreType.DMA],
        compiler_params=pltpu.CompilerParams(vmem_limit_bytes=1 << 20),
        name="prefetch",
    )(after, pltpu.with_memory_space_constraint(source, pltpu.HBM))


def add_body(one_ref, other_ref, out_ref):
    out_ref[...] = (one_ref[...].astype(f32) + other_ref[...].astype(f32)).astype(bf16)


def add(one, other):
    return local_call(add_body, "add", [(one.shape, bf16)], one, other)[0]


def ring_scatter(p1a, p1b, p2a, p2b, p3a, p3b, axis):
    ra = pp(p2a, axis, 1)
    rb = pp(p2b, axis, -1)
    t1 = pp(p1b, axis, 1)
    t3 = pp(p3a, axis, -1)
    s1 = pp(add(p1a, ra), axis, 1)
    s3 = pp(add(p3b, rb), axis, -1)
    return s1, t1, t3, s3


def join_body(p0, s1, t1, t3, s3, *outs):
    def rows(start, size):
        half, at = divmod(start, 32)
        one, other = ((s1, t3), (t1, s3))[half]
        window = pl.ds(at, size)
        total = p0[pl.ds(start, size), :].astype(f32) + one[window, :].astype(f32)
        return (total + other[window, :].astype(f32)).astype(bf16)

    for block in range(4):
        value = rows(block * 16, 16)
        if block == 0:
            outs[0][...] = value
        else:
            outs[2 * block - 1][...] = value[:8]
            outs[2 * block][...] = value[8:]


def scatter_tp(pieces):
    width = pieces[0].shape[1]
    moved = ring_scatter(*pieces[1:], "y")
    out = [((16, width), bf16)] + [((8, width), bf16)] * 6
    pieces = local_call(join_body, "join", out, pieces[0], *moved)
    return (pieces[0],) + ring_scatter(*pieces[1:], "zh")


def update_body(x_ref, p0, s1, t1, t3, s3, x_out):
    p0 = p0[...].astype(f32)
    upper = p0[:8] + s1[...].astype(f32) + t3[...].astype(f32)
    lower = p0[8:] + t1[...].astype(f32) + s3[...].astype(f32)
    x_out[:8] = x_ref[:8] + step_size * upper
    x_out[8:] = x_ref[8:] + step_size * lower


def norm_body(x_ref, gain_ref, a_out, b_out):
    x = x_ref[...]
    scale = lax.rsqrt(jnp.mean(x * x, axis=-1, keepdims=True) + eps_norm)
    h = (x * scale * gain_ref[...]).astype(bf16)
    a_out[...] = h[:8]
    b_out[...] = h[8:]


def exchange_kv(kv):
    other = pp(kv, "zl", 1)
    own_m1 = pp(kv, "x", 1)
    own_p1 = pp(kv, "x", -1)
    other_p1 = pp(other, "x", -1)
    other_m1 = pp(other, "x", 1)
    own_m2 = pp(own_m1, "x", 1)
    other_p2 = pp(other_p1, "x", -1)
    groups = [(kv, other), (own_m1, other_m1), (own_p1, other_p1), (own_m2, other_p2)]
    return [list(group) + [pp(piece, "c", 1) for piece in group] for group in groups]


def group_segments():
    x, zl, c = (lax.axis_index(name) for name in ("x", "zl", "c"))
    ids = []
    for dx in (0, 3, 1, 2):
        for dc in range(2):
            for dz in range(2):
                ids.append((x + dx) % 4 * 4 + (zl + dz) % 2 * 2 + (c + dc) % 2)
    return jnp.stack(ids).astype(jnp.int32)


def qkv_body(*refs):
    w_refs, (gain_ref, q_ref, kv_ref) = refs[8:11], refs[11:]
    h = jnp.concatenate([ref[...] for ref in refs[:8]], axis=0)
    for part in range(3):
        product = jnp.dot(h, w_refs[part][...], preferred_element_type=f32)
        if part == 2:
            kv_ref[:, pl.ds(2 * HD, 2 * HD)] = product.astype(bf16)
            continue
        for head in range(2):
            cols = pl.ds(head * HD, HD)
            value = product[:, head * HD : (head + 1) * HD]
            scale = lax.rsqrt(jnp.mean(value * value, axis=-1, keepdims=True) + eps_norm)
            value = (value * scale * gain_ref[part : part + 1, cols]).astype(bf16)
            if part == 0:
                q_ref[:, cols] = value
            else:
                kv_ref[:, cols] = value


def attend_group(first, ids_ref, len_ref, pos_ref, q_ref, pieces, top, acc):
    pos = pos_ref[...]
    own = ids_ref[0]
    valid = []
    for number in range(4):
        segment = ids_ref[4 * first + number]
        limit = jnp.where(segment <= own, len_ref[segment], 0)
        valid.append(pos < limit)
    valid = jnp.concatenate(valid, axis=1)
    ones = jnp.ones((4 * SEG, HD), bf16)
    for head in range(2):
        cols = pl.ds(head * HD, HD)
        keys = jnp.concatenate([piece[:, cols] for piece in pieces], axis=0)
        values = jnp.concatenate([piece[:, pl.ds((2 + head) * HD, HD)] for piece in pieces], axis=0)
        scores = lax.dot_general(
            q_ref[:, cols], keys, (((1,), (1,)), ((), ())), preferred_element_type=f32
        )
        scores = jnp.where(valid, scores * SCORE_SCALE, -1e30)
        best = jnp.max(scores, axis=-1, keepdims=True)
        if first > 0:
            before = top[head][:, :1]
            best = jnp.maximum(best, before)
            factor = jnp.exp2(before - best)
        weights = jnp.exp2(scores - best).astype(bf16)
        extended = jnp.concatenate([values, ones], axis=1)
        update = jnp.dot(weights, extended, preferred_element_type=f32)
        if first > 0:
            update = acc[head] * factor + update
        acc[head] = update
        top[head] = jnp.broadcast_to(best, (SEG, HD))


def attend_first_body(ids_ref, len_ref, pos_ref, q_ref, *refs):
    attend_group(0, ids_ref, len_ref, pos_ref, q_ref, refs[:4], *refs[4:])


def attend_rest_body(ids_ref, len_ref, pos_ref, q_ref, *refs):
    pieces, (w_ref, top_in, acc_in) = refs[:12], refs[12:15]
    outs, (top, acc) = refs[15:22], refs[22:]
    top[...] = top_in[...]
    acc[...] = acc_in[...]
    for first in range(1, 4):

        @pl.when(ids_ref[4 * first] < ids_ref[0])
        def _(first=first):
            group = pieces[4 * first - 4 : 4 * first]
            attend_group(first, ids_ref, len_ref, pos_ref, q_ref, group, top, acc)

    attended = jnp.concatenate(
        [(acc[head, :, :HD] / acc[head, :, HD:]).astype(bf16) for head in range(2)], axis=1
    )
    block = 1024
    for at in range(0, w_ref.shape[1], block):
        cols = pl.ds(at, block)
        partial = jnp.dot(attended, w_ref[:, cols], preferred_element_type=f32).astype(bf16)
        row = 0
        for out in outs:
            out[:, cols] = partial[row : row + out.shape[0]]
            row += out.shape[0]


def shards(states, norm_gain, qkv_weight, qk_gain, out_weight, segment_lengths):
    w = jnp.transpose(qkv_weight, (1, 0, 2))
    width = states.shape[1]
    y, zh = lax.axis_index("y"), lax.axis_index("zh")
    row = jnp.arange(SEG, dtype=jnp.int32)
    device = (y + row // 64) % 4 * 4 + (zh + row // 16 % 4) % 4
    pos = (device * ROWS + row % ROWS)[None, :]
    ids = group_segments()
    state = [((2, SEG, HD), f32), ((2, SEG, 2 * HD), f32)]
    scratch = [pltpu.VMEM(shape, dtype) for shape, dtype in state]
    partials = [((64, width), bf16)] + [((32, width), bf16)] * 6

    def one_step(step_index, current):
        half = ((ROWS // 2, width), bf16)
        h = local_call(norm_body, "norm", [half, half], current, norm_gain[None, :])
        projected = [((SEG, 2 * HD), bf16), ((SEG, 4 * HD), bf16)]
        weights = [prefetch(w, h[0], part) for part in range(3)]
        q, kv = local_call(qkv_body, "qkv", projected, *gather_tp(*h), *weights, qk_gain)
        groups = exchange_kv(kv)
        common = (ids, segment_lengths, pos, q)
        running = local_call(attend_first_body, "attend_own", state, *common, *groups[0])
        rest = groups[1] + groups[2] + groups[3]
        operands = (*common, *rest, prefetch(out_weight, kv), *running)
        pieces = local_call(attend_rest_body, "attend_rest", partials, *operands, scratch=scratch)
        out = [((ROWS, width), f32)]
        return local_call(update_body, "update", out, current, *scatter_tp(pieces))[0]

    return lax.fori_loop(0, STEPS, one_step, states)


def solution(mesh):
    inner = Mesh(mesh.devices.reshape(4, 2, 2, 4, 4), ("x", "zl", "c", "y", "zh"))
    tm, tp = ("x", "zl", "c"), ("y", "zh")
    return jax.shard_map(
        shards,
        mesh=inner,
        in_specs=(P(tm + tp, None), P(), P(None, None, tp), P(None, tp), P(tp, None), P()),
        out_specs=P(tm + tp, None),
        check_vma=False,
    )
```

```python
import jax
import jax.numpy as jnp
from jax import lax
from jax.experimental import pallas as pl
from jax.experimental.pallas import tpu as pltpu
from jax.sharding import Mesh, PartitionSpec as P

HD = 128
STEPS = 2
SEG = 256
ROWS = 16
eps_norm = 1e-06
step_size = -0.5
f32 = jnp.float32
bf16 = jnp.bfloat16
COLOR_AXES = (("zh", "y"), ("y", "zh"))
SCORE_SCALE = 1.4426950408889634 * HD ** (-0.5)


def color_widths(width):
    return (width - width // 4, width // 4)


def color_columns(width):
    first, second = color_widths(width)
    return (pl.ds(0, first), pl.ds(first, second))


def pp(value, axis, steps):
    count = lax.axis_size(axis)
    return lax.ppermute(value, axis, [(i, (i + steps) % count) for i in range(count)])


def ring_gather(a, b, axis):
    a_m1 = pp(a, axis, 1)
    b_p1 = pp(b, axis, -1)
    b_m1 = pp(b, axis, 1)
    a_p1 = pp(a, axis, -1)
    a_m2 = pp(a_m1, axis, 1)
    b_p2 = pp(b_p1, axis, -1)
    return (a, b, a_p1, b_p1), (a_m2, b_p2, a_m1, b_m1)


def gather_tp(a, b, axes):
    first, second = ring_gather(a, b, axes[0])
    first, second = ring_gather(jnp.concatenate(first, 0), jnp.concatenate(second, 0), axes[1])
    return first + second


def held(*arrays):
    return [pltpu.with_memory_space_constraint(value, pltpu.VMEM) for value in arrays]


def local_call(body, name, out, *operands, scratch=()):
    vmem = pl.BlockSpec(memory_space=pltpu.VMEM)
    smem = pl.BlockSpec(memory_space=pltpu.SMEM)
    small = [value.ndim == 1 for value in operands]
    return pl.pallas_call(
        body,
        in_specs=[smem if is_small else vmem for is_small in small],
        out_specs=[vmem] * len(out),
        out_shape=[pltpu.VMEM(shape, dtype) for shape, dtype in out],
        scratch_shapes=scratch,
        compiler_params=pltpu.CompilerParams(vmem_limit_bytes=24 << 20),
        name=name,
    )(*[value if is_small else held(value)[0] for value, is_small in zip(operands, small)])


def prefetch(source, after, part=None):
    def body(after_ref, source_ref, out_ref, arrived):
        del after_ref
        taken = source_ref if part is None else source_ref.at[part]
        copy = pltpu.make_async_copy(taken, out_ref, arrived)
        copy.start()
        copy.wait()

    shape = source.shape if part is None else source.shape[1:]
    anywhere = pl.BlockSpec(memory_space=pl.ANY)
    return pl.pallas_call(
        body,
        in_specs=[anywhere, anywhere],
        out_specs=pl.BlockSpec(memory_space=pltpu.VMEM),
        out_shape=pltpu.VMEM(shape, source.dtype),
        scratch_shapes=[pltpu.SemaphoreType.DMA],
        compiler_params=pltpu.CompilerParams(vmem_limit_bytes=1 << 20),
        name="prefetch",
    )(after, pltpu.with_memory_space_constraint(source, pltpu.HBM))


def add_body(one_ref, other_ref, out_ref):
    out_ref[...] = (one_ref[...].astype(f32) + other_ref[...].astype(f32)).astype(bf16)


def add(one, other):
    return local_call(add_body, "add", [(one.shape, bf16)], one, other)[0]


def ring_scatter(p1a, p1b, p2a, p2b, p3a, p3b, axis):
    ra = pp(p2a, axis, 1)
    rb = pp(p2b, axis, -1)
    t1 = pp(p1b, axis, 1)
    t3 = pp(p3a, axis, -1)
    s1 = pp(add(p1a, ra), axis, 1)
    s3 = pp(add(p3b, rb), axis, -1)
    return s1, t1, t3, s3


def join_body(p0, s1, t1, t3, s3, *outs):
    def rows(start, size):
        half, at = divmod(start, 32)
        one, other = ((s1, t3), (t1, s3))[half]
        window = pl.ds(at, size)
        total = p0[pl.ds(start, size), :].astype(f32) + one[window, :].astype(f32)
        return (total + other[window, :].astype(f32)).astype(bf16)

    for block in range(4):
        value = rows(block * 16, 16)
        if block == 0:
            outs[0][...] = value
        else:
            outs[2 * block - 1][...] = value[:8]
            outs[2 * block][...] = value[8:]


def scatter_tp(pieces, axes):
    width = pieces[0].shape[1]
    moved = ring_scatter(*pieces[1:], axes[0])
    out = [((16, width), bf16)] + [((8, width), bf16)] * 6
    pieces = local_call(join_body, "join", out, pieces[0], *moved)
    return (pieces[0],) + ring_scatter(*pieces[1:], axes[1])


def update_body(x_ref, *refs):
    x_out = refs[10]
    for color, cols in enumerate(color_columns(x_ref.shape[1])):
        p0, s1, t1, t3, s3 = (ref[...].astype(f32) for ref in refs[5 * color : 5 * color + 5])
        x_out[:8, cols] = x_ref[:8, cols] + step_size * (p0[:8] + s1 + t3)
        x_out[8:, cols] = x_ref[8:, cols] + step_size * (p0[8:] + t1 + s3)


def norm_body(x_ref, gain_ref, *outs):
    x = x_ref[...]
    scale = lax.rsqrt(jnp.mean(x * x, axis=-1, keepdims=True) + eps_norm)
    for color, cols in enumerate(color_columns(x_ref.shape[1])):
        h = (x_ref[:, cols] * scale * gain_ref[:, cols]).astype(bf16)
        outs[2 * color][...] = h[:8]
        outs[2 * color + 1][...] = h[8:]


def exchange_kv(kv):
    other = pp(kv, "zl", 1)
    own_m1 = pp(kv, "x", 1)
    own_p1 = pp(kv, "x", -1)
    other_p1 = pp(other, "x", -1)
    other_m1 = pp(other, "x", 1)
    own_m2 = pp(own_m1, "x", 1)
    other_p2 = pp(other_p1, "x", -1)
    groups = [(kv, other), (own_m1, other_m1, own_p1, other_p1), (own_m2, other_p2)]
    groups = [jnp.concatenate(group, 0) for group in groups]
    return [(group, pp(group, "c", 1)) for group in groups]


def group_segments():
    x, zl, c = (lax.axis_index(name) for name in ("x", "zl", "c"))
    ids = []
    for dx in (0, 3, 1, 2):
        for dc in range(2):
            for dz in range(2):
                ids.append((x + dx) % 4 * 4 + (zl + dz) % 2 * 2 + (c + dc) % 2)
    return jnp.stack(ids).astype(jnp.int32)


def qkv_body(*refs):
    w_refs, (gain_ref, q_ref, kv_ref) = refs[16:19], refs[19:]
    wide = jnp.concatenate([ref[...] for ref in refs[:8]], axis=0)
    rows = []
    for block in range(16):
        y, z = divmod(block, 4)
        half, at = divmod(y, 2)
        rows.append(refs[8 + 2 * z + half][pl.ds(16 * at, 16), :])
    narrow = jnp.concatenate(rows, axis=0)
    split = wide.shape[1]
    for part in range(3):
        product = jnp.dot(wide, w_refs[part][:split], preferred_element_type=f32)
        product += jnp.dot(narrow, w_refs[part][split:], preferred_element_type=f32)
        if part == 2:
            kv_ref[:, pl.ds(2 * HD, 2 * HD)] = product.astype(bf16)
            continue
        for head in range(2):
            cols = pl.ds(head * HD, HD)
            value = product[:, head * HD : (head + 1) * HD]
            scale = lax.rsqrt(jnp.mean(value * value, axis=-1, keepdims=True) + eps_norm)
            value = (value * scale * gain_ref[part : part + 1, cols]).astype(bf16)
            if part == 0:
                q_ref[:, cols] = value
            else:
                kv_ref[:, cols] = value


def attend_group(first, ids_ref, len_ref, pos_ref, q_ref, pieces, top, acc):
    pos = pos_ref[...]
    own = ids_ref[0]
    valid = []
    for number in range(4):
        segment = ids_ref[4 * first + number]
        limit = jnp.where(segment <= own, len_ref[segment], 0)
        valid.append(pos < limit)
    valid = jnp.concatenate(valid, axis=1)
    ones = jnp.ones((4 * SEG, HD), bf16)
    for head in range(2):
        cols = pl.ds(head * HD, HD)
        keys = jnp.concatenate([ref[rows, cols] for ref, rows in pieces], axis=0)
        value_cols = pl.ds((2 + head) * HD, HD)
        values = jnp.concatenate([ref[rows, value_cols] for ref, rows in pieces], axis=0)
        scores = lax.dot_general(
            q_ref[:, cols], keys, (((1,), (1,)), ((), ())), preferred_element_type=f32
        )
        scores = jnp.where(valid, scores * SCORE_SCALE, -1e30)
        best = jnp.max(scores, axis=-1, keepdims=True)
        if first > 0:
            before = top[head][:, :1]
            best = jnp.maximum(best, before)
            factor = jnp.exp2(before - best)
        weights = jnp.exp2(scores - best).astype(bf16)
        extended = jnp.concatenate([values, ones], axis=1)
        update = jnp.dot(weights, extended, preferred_element_type=f32)
        if first > 0:
            update = acc[head] * factor + update
        acc[head] = update
        top[head] = jnp.broadcast_to(best, (SEG, HD))


def windows(refs, start):
    return [(ref, pl.ds(start, 2 * SEG)) for ref in refs]


def attend_first_body(ids_ref, len_ref, pos_ref, q_ref, *refs):
    attend_group(0, ids_ref, len_ref, pos_ref, q_ref, windows(refs[:2], 0), *refs[2:])


def attend_rest_body(ids_ref, len_ref, pos_ref, q_ref, *refs):
    near, far, (w_ref, top_in, acc_in) = refs[:2], refs[2:4], refs[4:7]
    outs, (top, acc) = refs[7:21], refs[21:]
    top[...] = top_in[...]
    acc[...] = acc_in[...]
    groups = (windows(near, 0), windows(near, 2 * SEG), windows(far, 0))
    for first, group in enumerate(groups, 1):

        @pl.when(ids_ref[4 * first] < ids_ref[0])
        def _(first=first, group=group):
            attend_group(first, ids_ref, len_ref, pos_ref, q_ref, group, top, acc)

    attended = jnp.concatenate(
        [(acc[head, :, :HD] / acc[head, :, HD:]).astype(bf16) for head in range(2)], axis=1
    )
    width = w_ref.shape[1]
    block = width // 4
    for at in range(4):
        cols = pl.ds(at * block, block)
        partial = jnp.dot(attended, w_ref[:, cols], preferred_element_type=f32).astype(bf16)
        color, inside = (0, cols) if at < 3 else (1, pl.ds(0, block))
        if color == 1:
            blocks = [partial[16 * (4 * y + z) : 16 * (4 * y + z) + 16] for z in range(4) for y in range(4)]
            partial = jnp.concatenate(blocks, axis=0)
        row = 0
        for out in outs[7 * color : 7 * color + 7]:
            out[:, inside] = partial[row : row + out.shape[0]]
            row += out.shape[0]


def shards(states, norm_gain, qkv_weight, qk_gain, out_weight, segment_lengths):
    w = jnp.transpose(qkv_weight, (1, 0, 2))
    width = states.shape[1]
    y, zh = lax.axis_index("y"), lax.axis_index("zh")
    row = jnp.arange(SEG, dtype=jnp.int32)
    device = (y + row // 64) % 4 * 4 + (zh + row // 16 % 4) % 4
    pos = (device * ROWS + row % ROWS)[None, :]
    ids = group_segments()
    state = [((2, SEG, HD), f32), ((2, SEG, 2 * HD), f32)]
    scratch = [pltpu.VMEM(shape, dtype) for shape, dtype in state]
    partials, halves = [], []
    for size in color_widths(width):
        partials += [((64, size), bf16)] + [((32, size), bf16)] * 6
        halves += [((ROWS // 2, size), bf16)] * 2

    def one_step(step_index, current):
        h = local_call(norm_body, "norm", halves, current, norm_gain[None, :])
        gathered = gather_tp(*h[:2], COLOR_AXES[0]) + gather_tp(*h[2:], COLOR_AXES[1])
        projected = [((SEG, 2 * HD), bf16), ((SEG, 4 * HD), bf16)]
        weights = [prefetch(w, h[0], part) for part in range(3)]
        q, kv = local_call(qkv_body, "qkv", projected, *gathered, *weights, qk_gain)
        groups = exchange_kv(kv)
        common = (ids, segment_lengths, pos, q)
        running = local_call(attend_first_body, "attend_own", state, *common, *groups[0])
        operands = (*common, *groups[1], *groups[2], prefetch(out_weight, kv), *running)
        pieces = local_call(attend_rest_body, "attend_rest", partials, *operands, scratch=scratch)
        moved = scatter_tp(pieces[:7], COLOR_AXES[0][::-1]) + scatter_tp(pieces[7:], COLOR_AXES[1][::-1])
        return local_call(update_body, "update", [((ROWS, width), f32)], current, *moved)[0]

    return lax.fori_loop(0, STEPS, one_step, states)


def solution(mesh):
    inner = Mesh(mesh.devices.reshape(4, 2, 2, 4, 4), ("x", "zl", "c", "y", "zh"))
    tm, tp = ("x", "zl", "c"), ("y", "zh")
    return jax.shard_map(
        shards,
        mesh=inner,
        in_specs=(P(tm + tp, None), P(), P(None, None, tp), P(None, tp), P(tp, None), P()),
        out_specs=P(tm + tp, None),
        check_vma=False,
    )
```

```python
import jax
import jax.numpy as jnp
from jax import lax
from jax.experimental import pallas as pl
from jax.experimental.pallas import tpu as pltpu
from jax.sharding import Mesh, PartitionSpec as P


HD = 128
STEPS = 2
SEG = 256
ROWS = 16
eps_norm = 1e-06
step_size = -0.5
f32 = jnp.float32
bf16 = jnp.bfloat16
SCORE_SCALE = 1.4426950408889634 * HD ** (-0.5)


def pp(value, axis, steps):
    count = lax.axis_size(axis)
    return lax.ppermute(value, axis, [(i, (i + steps) % count) for i in range(count)])


def gather_tp(h):
    half = ROWS // 2
    b1 = pp(h, "zh", -1)
    b3 = pp(h, "zh", 1)
    b2_a = pp(b3[:half], "zh", 1)
    b2_b = pp(b1[half:], "zh", -1)
    a = jnp.concatenate([h, b1], 0)
    b = jnp.concatenate([b2_a, b2_b, b3], 0)
    a_m1 = pp(a, "y", 1)
    a_p1 = pp(a, "y", -1)
    b_p1 = pp(b, "y", -1)
    b_m1 = pp(b, "y", 1)
    a_m2 = pp(a_m1, "y", 1)
    b_p2 = pp(b_p1, "y", -1)
    return a, b, a_p1, b_p1, a_m2, b_p2, a_m1, b_m1


def held(*arrays):
    return [pltpu.with_memory_space_constraint(value, pltpu.VMEM) for value in arrays]


def local_call(body, out, *operands, scratch=()):
    vmem = pl.BlockSpec(memory_space=pltpu.VMEM)
    smem = pl.BlockSpec(memory_space=pltpu.SMEM)
    small = [value.ndim == 1 for value in operands]
    operands = [value if is_small else held(value)[0] for value, is_small in zip(operands, small)]
    return pl.pallas_call(
        body,
        in_specs=[smem if is_small else vmem for is_small in small],
        out_specs=[vmem] * len(out),
        out_shape=[pltpu.VMEM(shape, dtype) for shape, dtype in out],
        scratch_shapes=scratch,
        compiler_params=pltpu.CompilerParams(vmem_limit_bytes=24 << 20),
    )(*operands)


def prefetch(source, after, part=None):
    def body(after_ref, source_ref, out_ref, arrived):
        del after_ref
        taken = source_ref if part is None else source_ref.at[part]
        copy = pltpu.make_async_copy(taken, out_ref, arrived)
        copy.start()
        copy.wait()

    shape = source.shape if part is None else source.shape[1:]
    anywhere = pl.BlockSpec(memory_space=pl.ANY)
    return pl.pallas_call(
        body,
        in_specs=[anywhere, anywhere],
        out_specs=pl.BlockSpec(memory_space=pltpu.VMEM),
        out_shape=pltpu.VMEM(shape, source.dtype),
        scratch_shapes=[pltpu.SemaphoreType.DMA],
        compiler_params=pltpu.CompilerParams(vmem_limit_bytes=1 << 20),
        name="prefetch",
    )(after, pltpu.with_memory_space_constraint(source, pltpu.HBM))


def add_body(one_ref, other_ref, out_ref):
    out_ref[...] = (one_ref[...].astype(f32) + other_ref[...].astype(f32)).astype(bf16)


def add(one, other):
    return local_call(add_body, [(one.shape, bf16)], one, other)[0]


Z_ORDER = (2, 1, 3, 0)


def y_sum(start, size, p0, one, other):
    at = pl.ds(start % 32, size)
    total = p0[pl.ds(start, size), :].astype(f32) + one[at, :].astype(f32)
    return total + other[at, :].astype(f32)


def opposite_body(p0, s1, t3, z2a, z2b):
    total = y_sum(0, 16, p0, s1, t3).astype(bf16)
    z2a[...] = total[:8]
    z2b[...] = total[8:]


def right_body(p0, s1, t3, from_left, out):
    total = y_sum(16, 16, p0, s1, t3)
    out[:8] = (total[:8] + from_left[...].astype(f32)).astype(bf16)
    out[8:] = total[8:].astype(bf16)


def left_body(p0, t1, s3, from_right, out):
    total = y_sum(32, 16, p0, t1, s3)
    out[:8] = total[:8].astype(bf16)
    out[8:] = (total[8:] + from_right[...].astype(f32)).astype(bf16)


def scatter_tp(p0, p1a, p1b, p2a, p2b, p3a, p3b):
    width = p0.shape[1]
    block, half = [((ROWS, width), bf16)], [((ROWS // 2, width), bf16)]
    ra = pp(p2a, "y", 1)
    rb = pp(p2b, "y", -1)
    t3 = pp(p3a, "y", -1)
    s1 = pp(add(p1a, ra), "y", 1)
    t1 = pp(p1b, "y", 1)
    s3 = pp(add(p3b, rb), "y", -1)
    z2a, z2b = local_call(opposite_body, half * 2, p0, s1, t3)
    from_left = pp(z2a, "zh", 1)
    from_right = pp(z2b, "zh", -1)
    z1 = local_call(right_body, block, p0, s1, t3, from_left)[0]
    r1 = pp(z1, "zh", 1)
    z3 = local_call(left_body, block, p0, t1, s3, from_right)[0]
    r3 = pp(z3, "zh", -1)
    return p0, t1, s3, r1, r3


def update_body(x_ref, p0, t1, s3, r1, r3, x_out):
    total = y_sum(48, 16, p0, t1, s3) + r1[...].astype(f32) + r3[...].astype(f32)
    x_out[...] = x_ref[...] + step_size * total


def norm_body(x_ref, gain_ref, h_out):
    x = x_ref[...]
    scale = lax.rsqrt(jnp.mean(x * x, axis=-1, keepdims=True) + eps_norm)
    h_out[...] = (x * scale * gain_ref[...]).astype(bf16)


def exchange_kv(kv):
    other = pp(kv, "zl", 1)
    own_p1 = pp(kv, "x", -1)
    own_m1 = pp(kv, "x", 1)
    other_p1 = pp(other, "x", -1)
    other_m1 = pp(other, "x", 1)
    own_m2 = pp(own_m1, "x", 1)
    other_p2 = pp(other_p1, "x", -1)
    return (kv, other), (own_m1, other_m1, own_p1, other_p1), (own_m2, other_p2)


def group_segments():
    x, zl, c = (lax.axis_index(name) for name in ("x", "zl", "c"))
    ids = []
    for dx in (0, 3, 1, 2):
        for dz in range(2):
            for dc in range(2):
                ids.append((x + dx) % 4 * 4 + (zl + dz) % 2 * 2 + (c + dc) % 2)
    return jnp.stack(ids).astype(jnp.int32)


def qkv_body(ids_ref, *refs):
    w_refs, (gain_ref, kv_ref, q_ref, send_ref) = refs[8:11], refs[11:]
    h = jnp.concatenate([ref[...] for ref in refs[:8]], axis=0)
    first = ids_ref[0] % 2 == 0
    for part in range(3):
        product = jnp.dot(h, w_refs[part][...], preferred_element_type=f32)
        heads = []
        for head in range(2):
            value = product[:, head * HD : (head + 1) * HD]
            if part < 2:
                gain = gain_ref[part : part + 1, pl.ds(head * HD, HD)]
                scale = lax.rsqrt(jnp.mean(value * value, axis=-1, keepdims=True) + eps_norm)
                value = value * scale * gain
            heads.append(value)
        own = jnp.where(first, heads[0], heads[1]).astype(bf16)
        other = jnp.where(first, heads[1], heads[0]).astype(bf16)
        at = (2, 0, 1)[part]
        send_ref[:, pl.ds(at * HD, HD)] = other
        if part == 0:
            q_ref[...] = own
        else:
            kv_ref[:, pl.ds(at * HD, HD)] = own


def attend_group(first, ids_ref, len_ref, pos_ref, queries, pieces, top, acc):
    pos = pos_ref[...]
    ones = jnp.ones((4 * SEG, HD), bf16)
    keys = jnp.concatenate([piece[:, :HD] for piece in pieces], axis=0)
    values = jnp.concatenate([piece[:, HD:] for piece in pieces], axis=0)
    extended = jnp.concatenate([values, ones], axis=1)
    for half in range(2):
        valid = []
        for number in range(4):
            segment = ids_ref[4 * first + number]
            limit = jnp.where(segment <= ids_ref[half], len_ref[segment], 0)
            valid.append(pos < limit)
        valid = jnp.concatenate(valid, axis=1)
        scores = lax.dot_general(
            queries[half], keys, (((1,), (1,)), ((), ())), preferred_element_type=f32
        )
        scores = jnp.where(valid, scores * SCORE_SCALE, -1e30)
        best = jnp.max(scores, axis=-1, keepdims=True)
        if first > 0:
            before = top[half][:, :1]
            best = jnp.maximum(best, before)
            factor = jnp.exp2(before - best)
        weights = jnp.exp2(scores - best).astype(bf16)
        update = jnp.dot(weights, extended, preferred_element_type=f32)
        if first > 0:
            update = acc[half] * factor + update
        acc[half] = update
        top[half] = jnp.broadcast_to(best, (SEG, HD))


def queries_of(q_ref, got_ref):
    return q_ref[...], got_ref[:, pl.ds(2 * HD, HD)]


def attend_own_body(ids_ref, len_ref, pos_ref, q_ref, got_ref, *refs):
    queries = queries_of(q_ref, got_ref)
    attend_group(0, ids_ref, len_ref, pos_ref, queries, refs[:2], *refs[2:])


def attend_near_body(ids_ref, len_ref, pos_ref, q_ref, got_ref, *refs):
    pieces, (top_in, acc_in, top, acc) = refs[:4], refs[4:]
    top[...] = top_in[...]
    acc[...] = acc_in[...]
    for first in (1, 2):

        @pl.when(ids_ref[4 * first] < ids_ref[0])
        def _(first=first):
            queries = queries_of(q_ref, got_ref)
            group = pieces[2 * first - 2 : 2 * first]
            attend_group(first, ids_ref, len_ref, pos_ref, queries, group, top, acc)


def attend_far_body(ids_ref, len_ref, pos_ref, q_ref, got_ref, *refs):
    pieces, (top_in, acc_in), outs, (top, acc) = refs[:2], refs[2:4], refs[4:6], refs[6:]
    top[...] = top_in[...]
    acc[...] = acc_in[...]

    @pl.when(ids_ref[12] < ids_ref[0])
    def _():
        queries = queries_of(q_ref, got_ref)
        attend_group(3, ids_ref, len_ref, pos_ref, queries, pieces, top, acc)

    for half, out in enumerate(outs):
        out[...] = (acc[half, :, :HD] / acc[half, :, HD:]).astype(bf16)


def project_body(ids_ref, own_ref, other_ref, w_ref, *outs):
    own, other = own_ref[...], other_ref[...]
    first = ids_ref[0] % 2 == 0
    attended = jnp.where(
        first, jnp.concatenate([own, other], axis=1), jnp.concatenate([other, own], axis=1)
    )
    order = [4 * y + z for y in range(4) for z in Z_ORDER]
    attended = jnp.concatenate([attended[16 * at : 16 * at + 16] for at in order], axis=0)
    block = 1024
    for at in range(0, w_ref.shape[1], block):
        cols = pl.ds(at, block)
        partial = jnp.dot(attended, w_ref[:, cols], preferred_element_type=f32).astype(bf16)
        row = 0
        for out in outs:
            out[:, cols] = partial[row : row + out.shape[0]]
            row += out.shape[0]


def shards(states, norm_gain, qkv_weight, qk_gain, out_weight, segment_lengths):
    w = jnp.transpose(qkv_weight, (1, 0, 2))
    width = states.shape[1]
    y, zh = lax.axis_index("y"), lax.axis_index("zh")
    row = jnp.arange(SEG, dtype=jnp.int32)
    device = (y + row // 64) % 4 * 4 + (zh + row // 16 % 4) % 4
    pos = (device * ROWS + row % ROWS)[None, :]
    ids = group_segments()
    state = [((2, SEG, HD), f32), ((2, SEG, 2 * HD), f32)]
    scratch = [pltpu.VMEM(shape, dtype) for shape, dtype in state]
    partials = [((64, width), bf16)] + [((32, width), bf16)] * 6
    projected = [((SEG, cols * HD), bf16) for cols in (2, 1, 3)]
    columns = [((SEG, HD), bf16)] * 2

    def one_step(step_index, current):
        h = local_call(norm_body, [((ROWS, width), bf16)], current, norm_gain[None, :])[0]
        weights = [prefetch(w, h, part) for part in range(3)]
        w_out = prefetch(out_weight, h)
        operands = (ids, *gather_tp(h), *weights, qk_gain)
        kv, q, send = local_call(qkv_body, projected, *operands)
        got = pp(send, "c", 1)
        own, near, far = exchange_kv(jnp.concatenate([kv, got[:, : 2 * HD]], 0))
        common = (ids, segment_lengths, pos, q, got)
        running = local_call(attend_own_body, state, *common, *own)
        running = local_call(attend_near_body, state, *common, *near, *running)
        mine, others = local_call(
            attend_far_body, columns, *common, *far, *running, scratch=scratch
        )
        operands = (ids, mine, pp(others, "c", 1), w_out)
        moved = scatter_tp(*local_call(project_body, partials, *operands))
        return local_call(update_body, [((ROWS, width), f32)], current, *moved)[0]

    return lax.fori_loop(0, STEPS, one_step, states)


def solution(mesh):
    inner = Mesh(mesh.devices.reshape(4, 2, 2, 4, 4), ("x", "zl", "c", "y", "zh"))
    tm, tp = ("x", "zl", "c"), ("y", "zh")
    return jax.shard_map(
        shards,
        mesh=inner,
        in_specs=(P(tm + tp, None), P(), P(None, None, tp), P(None, tp), P(tp, None), P()),
        out_specs=P(tm + tp, None),
        check_vma=False,
    )
```

```python
import jax
import jax.numpy as jnp
from jax import lax
from jax.experimental import pallas as pl
from jax.experimental.pallas import tpu as pltpu
from jax.sharding import Mesh, PartitionSpec as P


HD = 128
STEPS = 2
SEG = 256
ROWS = 16
eps_norm = 1e-06
step_size = -0.5
f32 = jnp.float32
bf16 = jnp.bfloat16
SCORE_SCALE = 1.4426950408889634 * HD ** (-0.5)


def pp(value, axis, steps):
    count = lax.axis_size(axis)
    return lax.ppermute(value, axis, [(i, (i + steps) % count) for i in range(count)])


G_ORDER = (0, 1, 3, 2)


def gather_tp(h):
    half = ROWS // 2
    b1 = pp(h, "zh", -1)
    b3 = pp(h, "zh", 1)
    own_p1 = pp(h, "y", -1)
    own_m1 = pp(h, "y", 1)
    b2_a = pp(b3[:half], "zh", 1)
    b2_b = pp(b1[half:], "zh", -1)
    own_m2 = pp(own_m1, "y", 1)
    mid = jnp.concatenate([b1, b3], 0)
    mid_p1 = pp(mid, "y", -1)
    mid_m1 = pp(mid, "y", 1)
    last = jnp.concatenate([b2_a, b2_b], 0)
    last_p1 = pp(last, "y", -1)
    last_m1 = pp(last, "y", 1)
    mid_p2 = pp(mid_p1[ROWS:], "y", -1)
    mid_m2 = pp(mid_m1[:ROWS], "y", 1)
    last_p2 = pp(last_p1, "y", -1)
    near = (h, mid, last, own_p1, mid_p1, last_p1)
    return near + (own_m2, mid_m2, mid_p2, last_p2, own_m1, mid_m1, last_m1)


def held(*arrays):
    return [pltpu.with_memory_space_constraint(value, pltpu.VMEM) for value in arrays]


def local_call(body, out, *operands, scratch=()):
    vmem = pl.BlockSpec(memory_space=pltpu.VMEM)
    smem = pl.BlockSpec(memory_space=pltpu.SMEM)
    small = [value.ndim == 1 for value in operands]
    operands = [value if is_small else held(value)[0] for value, is_small in zip(operands, small)]
    return pl.pallas_call(
        body,
        in_specs=[smem if is_small else vmem for is_small in small],
        out_specs=[vmem] * len(out),
        out_shape=[pltpu.VMEM(shape, dtype) for shape, dtype in out],
        scratch_shapes=scratch,
        compiler_params=pltpu.CompilerParams(vmem_limit_bytes=24 << 20),
    )(*operands)


def prefetch(source, after, part=None):
    def body(after_ref, source_ref, out_ref, arrived):
        del after_ref
        taken = source_ref if part is None else source_ref.at[part]
        copy = pltpu.make_async_copy(taken, out_ref, arrived)
        copy.start()
        copy.wait()

    shape = source.shape if part is None else source.shape[1:]
    anywhere = pl.BlockSpec(memory_space=pl.ANY)
    return pl.pallas_call(
        body,
        in_specs=[anywhere, anywhere],
        out_specs=pl.BlockSpec(memory_space=pltpu.VMEM),
        out_shape=pltpu.VMEM(shape, source.dtype),
        scratch_shapes=[pltpu.SemaphoreType.DMA],
        compiler_params=pltpu.CompilerParams(vmem_limit_bytes=1 << 20),
        name="prefetch",
    )(after, pltpu.with_memory_space_constraint(source, pltpu.HBM))


def add_body(one_ref, other_ref, out_ref):
    out_ref[...] = (one_ref[...].astype(f32) + other_ref[...].astype(f32)).astype(bf16)


def add(one, other):
    return local_call(add_body, [(one.shape, bf16)], one, other)[0]


Z_ORDER = (2, 1, 3, 0)


def y_sum(start, size, p0, one, other):
    at = pl.ds(start % 32, size)
    total = p0[pl.ds(start, size), :].astype(f32) + one[at, :].astype(f32)
    return total + other[at, :].astype(f32)


def opposite_body(p0, s1, t3, z2a, z2b):
    total = y_sum(0, 16, p0, s1, t3).astype(bf16)
    z2a[...] = total[:8]
    z2b[...] = total[8:]


def right_body(p0, s1, t3, from_left, out):
    total = y_sum(16, 16, p0, s1, t3)
    out[:8] = (total[:8] + from_left[...].astype(f32)).astype(bf16)
    out[8:] = total[8:].astype(bf16)


def left_body(p0, t1, s3, from_right, out):
    total = y_sum(32, 16, p0, t1, s3)
    out[:8] = total[:8].astype(bf16)
    out[8:] = (total[8:] + from_right[...].astype(f32)).astype(bf16)


def scatter_tp(p0, p1a, p1b, p2a, p2b, p3a, p3b):
    width = p0.shape[1]
    block, half = [((ROWS, width), bf16)], [((ROWS // 2, width), bf16)]
    ra = pp(p2a, "y", 1)
    rb = pp(p2b, "y", -1)
    t3 = pp(p3a, "y", -1)
    s1 = pp(add(p1a, ra), "y", 1)
    t1 = pp(p1b, "y", 1)
    s3 = pp(add(p3b, rb), "y", -1)
    z2a, z2b = local_call(opposite_body, half * 2, p0, s1, t3)
    from_left = pp(z2a, "zh", 1)
    from_right = pp(z2b, "zh", -1)
    z1 = local_call(right_body, block, p0, s1, t3, from_left)[0]
    r1 = pp(z1, "zh", 1)
    z3 = local_call(left_body, block, p0, t1, s3, from_right)[0]
    r3 = pp(z3, "zh", -1)
    return p0, t1, s3, r1, r3


def update_body(x_ref, p0, t1, s3, r1, r3, x_out):
    total = y_sum(48, 16, p0, t1, s3) + r1[...].astype(f32) + r3[...].astype(f32)
    x_out[...] = x_ref[...] + step_size * total


def norm_body(x_ref, gain_ref, h_out):
    x = x_ref[...]
    scale = lax.rsqrt(jnp.mean(x * x, axis=-1, keepdims=True) + eps_norm)
    h_out[...] = (x * scale * gain_ref[...]).astype(bf16)


def exchange_kv(kv):
    other = pp(kv, "zl", 1)
    own_p1 = pp(kv, "x", -1)
    own_m1 = pp(kv, "x", 1)
    other_p1 = pp(other, "x", -1)
    own_m2 = pp(own_m1, "x", 1)
    other_m1 = pp(own_m1, "zl", 1)
    other_p2a = pp(other_p1[:SEG], "x", -1)
    other_p2b = pp(own_m2[SEG:], "zl", 1)
    other_p2 = jnp.concatenate([other_p2a, other_p2b], 0)
    return (kv, other), (own_m1, other_m1, own_p1, other_p1), (own_m2, other_p2)


def group_segments():
    x, zl, c = (lax.axis_index(name) for name in ("x", "zl", "c"))
    ids = []
    for dx in (0, 3, 1, 2):
        for dz in range(2):
            for dc in range(2):
                ids.append((x + dx) % 4 * 4 + (zl + dz) % 2 * 2 + (c + dc) % 2)
    return jnp.stack(ids).astype(jnp.int32)


def qkv_body(ids_ref, *refs):
    w_refs, (gain_ref, kv_ref, q_ref, send_ref) = refs[13:16], refs[16:]
    h = jnp.concatenate([ref[...] for ref in refs[:13]], axis=0)
    first = ids_ref[0] % 2 == 0
    for part in range(3):
        product = jnp.dot(h, w_refs[part][...], preferred_element_type=f32)
        heads = []
        for head in range(2):
            value = product[:, head * HD : (head + 1) * HD]
            if part < 2:
                gain = gain_ref[part : part + 1, pl.ds(head * HD, HD)]
                scale = lax.rsqrt(jnp.mean(value * value, axis=-1, keepdims=True) + eps_norm)
                value = value * scale * gain
            heads.append(value)
        own = jnp.where(first, heads[0], heads[1]).astype(bf16)
        other = jnp.where(first, heads[1], heads[0]).astype(bf16)
        at = (2, 0, 1)[part]
        send_ref[:, pl.ds(at * HD, HD)] = other
        if part == 0:
            q_ref[...] = own
        else:
            kv_ref[:, pl.ds(at * HD, HD)] = own


def attend_group(first, ids_ref, len_ref, pos_ref, queries, pieces, top, acc):
    pos = pos_ref[...]
    ones = jnp.ones((4 * SEG, HD), bf16)
    keys = jnp.concatenate([piece[:, :HD] for piece in pieces], axis=0)
    values = jnp.concatenate([piece[:, HD:] for piece in pieces], axis=0)
    extended = jnp.concatenate([values, ones], axis=1)
    for half in range(2):
        valid = []
        for number in range(4):
            segment = ids_ref[4 * first + number]
            limit = jnp.where(segment <= ids_ref[half], len_ref[segment], 0)
            valid.append(pos < limit)
        valid = jnp.concatenate(valid, axis=1)
        scores = lax.dot_general(
            queries[half], keys, (((1,), (1,)), ((), ())), preferred_element_type=f32
        )
        scores = jnp.where(valid, scores * SCORE_SCALE, -1e30)
        best = jnp.max(scores, axis=-1, keepdims=True)
        if first > 0:
            before = top[half][:, :1]
            best = jnp.maximum(best, before)
            factor = jnp.exp2(before - best)
        weights = jnp.exp2(scores - best).astype(bf16)
        update = jnp.dot(weights, extended, preferred_element_type=f32)
        if first > 0:
            update = acc[half] * factor + update
        acc[half] = update
        top[half] = jnp.broadcast_to(best, (SEG, HD))


def queries_of(q_ref, got_ref):
    return q_ref[...], got_ref[:, pl.ds(2 * HD, HD)]


def attend_own_body(ids_ref, len_ref, pos_ref, q_ref, got_ref, *refs):
    queries = queries_of(q_ref, got_ref)
    attend_group(0, ids_ref, len_ref, pos_ref, queries, refs[:2], *refs[2:])


def attend_near_body(ids_ref, len_ref, pos_ref, q_ref, got_ref, *refs):
    pieces, (top_in, acc_in, top, acc) = refs[:4], refs[4:]
    top[...] = top_in[...]
    acc[...] = acc_in[...]
    for first in (1, 2):

        @pl.when(ids_ref[4 * first] < ids_ref[0])
        def _(first=first):
            queries = queries_of(q_ref, got_ref)
            group = pieces[2 * first - 2 : 2 * first]
            attend_group(first, ids_ref, len_ref, pos_ref, queries, group, top, acc)


def attend_far_body(ids_ref, len_ref, pos_ref, q_ref, got_ref, *refs):
    pieces, (top_in, acc_in), outs, (top, acc) = refs[:2], refs[2:4], refs[4:6], refs[6:]
    top[...] = top_in[...]
    acc[...] = acc_in[...]

    @pl.when(ids_ref[12] < ids_ref[0])
    def _():
        queries = queries_of(q_ref, got_ref)
        attend_group(3, ids_ref, len_ref, pos_ref, queries, pieces, top, acc)

    for half, out in enumerate(outs):
        out[...] = (acc[half, :, :HD] / acc[half, :, HD:]).astype(bf16)


def project_body(ids_ref, own_ref, other_ref, w_ref, *outs):
    own, other = own_ref[...], other_ref[...]
    first = ids_ref[0] % 2 == 0
    attended = jnp.where(
        first, jnp.concatenate([own, other], axis=1), jnp.concatenate([other, own], axis=1)
    )
    order = [4 * y + G_ORDER.index(z) for y in range(4) for z in Z_ORDER]
    attended = jnp.concatenate([attended[16 * at : 16 * at + 16] for at in order], axis=0)
    block = 1024
    for at in range(0, w_ref.shape[1], block):
        cols = pl.ds(at, block)
        partial = jnp.dot(attended, w_ref[:, cols], preferred_element_type=f32).astype(bf16)
        row = 0
        for out in outs:
            out[:, cols] = partial[row : row + out.shape[0]]
            row += out.shape[0]


def shards(states, norm_gain, qkv_weight, qk_gain, out_weight, segment_lengths):
    w = jnp.transpose(qkv_weight, (1, 0, 2))
    width = states.shape[1]
    y, zh = lax.axis_index("y"), lax.axis_index("zh")
    row = jnp.arange(SEG, dtype=jnp.int32)
    at = row // 16 % 4
    z_block = sum(jnp.where(at == place, block, 0) for place, block in enumerate(G_ORDER))
    device = (y + row // 64) % 4 * 4 + (zh + z_block) % 4
    pos = (device * ROWS + row % ROWS)[None, :]
    ids = group_segments()
    state = [((2, SEG, HD), f32), ((2, SEG, 2 * HD), f32)]
    scratch = [pltpu.VMEM(shape, dtype) for shape, dtype in state]
    partials = [((64, width), bf16)] + [((32, width), bf16)] * 6
    projected = [((SEG, cols * HD), bf16) for cols in (2, 1, 3)]
    columns = [((SEG, HD), bf16)] * 2

    def one_step(step_index, current):
        h = local_call(norm_body, [((ROWS, width), bf16)], current, norm_gain[None, :])[0]
        weights = [prefetch(w, h, part) for part in range(3)]
        w_out = prefetch(out_weight, h)
        operands = (ids, *gather_tp(h), *weights, qk_gain)
        kv, q, send = local_call(qkv_body, projected, *operands)
        got = pp(send, "c", 1)
        own, near, far = exchange_kv(jnp.concatenate([kv, got[:, : 2 * HD]], 0))
        common = (ids, segment_lengths, pos, q, got)
        running = local_call(attend_own_body, state, *common, *own)
        running = local_call(attend_near_body, state, *common, *near, *running)
        mine, others = local_call(
            attend_far_body, columns, *common, *far, *running, scratch=scratch
        )
        operands = (ids, mine, pp(others, "c", 1), w_out)
        moved = scatter_tp(*local_call(project_body, partials, *operands))
        return local_call(update_body, [((ROWS, width), f32)], current, *moved)[0]

    return lax.fori_loop(0, STEPS, one_step, states)


def solution(mesh):
    inner = Mesh(mesh.devices.reshape(4, 2, 2, 4, 4), ("x", "zl", "c", "y", "zh"))
    tm, tp = ("x", "zl", "c"), ("y", "zh")
    return jax.shard_map(
        shards,
        mesh=inner,
        in_specs=(P(tm + tp, None), P(), P(None, None, tp), P(None, tp), P(tp, None), P()),
        out_specs=P(tm + tp, None),
        check_vma=False,
    )
```

```python
import jax
import jax.numpy as jnp
from jax import lax
from jax.experimental import pallas as pl
from jax.experimental.pallas import tpu as pltpu
from jax.sharding import Mesh, PartitionSpec as P


HD = 128
STEPS = 2
SEG = 256
ROWS = 16
eps_norm = 1e-06
step_size = -0.5
f32 = jnp.float32
bf16 = jnp.bfloat16
SCORE_SCALE = 1.4426950408889634 * HD ** (-0.5)


def pp(value, axis, steps):
    count = lax.axis_size(axis)
    return lax.ppermute(value, axis, [(i, (i + steps) % count) for i in range(count)])


G_ORDER = (0, 1, 3, 2)


def gather_tp(h):
    half = ROWS // 2
    b1 = pp(h, "zh", -1)
    b3 = pp(h, "zh", 1)
    own_p1 = pp(h, "y", -1)
    own_m1 = pp(h, "y", 1)
    b2_a = pp(b3[:half], "zh", 1)
    b2_b = pp(b1[half:], "zh", -1)
    own_m2 = pp(own_m1, "y", 1)
    mid = jnp.concatenate([b1, b3], 0)
    mid_p1 = pp(mid, "y", -1)
    mid_m1 = pp(mid, "y", 1)
    last = jnp.concatenate([b2_a, b2_b], 0)
    last_p1 = pp(last, "y", -1)
    last_m1 = pp(last, "y", 1)
    mid_p2 = pp(mid_p1[ROWS:], "y", -1)
    mid_m2 = pp(mid_m1[:ROWS], "y", 1)
    last_p2 = pp(last_p1, "y", -1)
    near = (h, mid, last, own_p1, mid_p1, last_p1)
    return near + (own_m2, mid_m2, mid_p2, last_p2, own_m1, mid_m1, last_m1)


def local_call(body, out, *operands, scratch=(), in_hbm=0):
    vmem = pl.BlockSpec(memory_space=pltpu.VMEM)
    smem = pl.BlockSpec(memory_space=pltpu.SMEM)
    anywhere = pl.BlockSpec(memory_space=pl.ANY)
    specs, values = [], []
    for number, value in enumerate(operands):
        if number >= len(operands) - in_hbm:
            specs.append(anywhere)
            value = pltpu.with_memory_space_constraint(value, pltpu.HBM)
        elif value.ndim == 1:
            specs.append(smem)
        else:
            specs.append(vmem)
            value = pltpu.with_memory_space_constraint(value, pltpu.VMEM)
        values.append(value)
    return pl.pallas_call(
        body,
        in_specs=specs,
        out_specs=[vmem] * len(out),
        out_shape=[pltpu.VMEM(shape, dtype) for shape, dtype in out],
        scratch_shapes=scratch,
        compiler_params=pltpu.CompilerParams(vmem_limit_bytes=24 << 20),
    )(*values)


def add(one, other, at):
    def body(one_ref, other_ref, out_ref):
        window = pl.ds(at, other.shape[0])
        if other.shape != one.shape:
            out_ref[...] = one_ref[...]
        out_ref[window, :] = (one_ref[window, :].astype(f32) + other_ref[...].astype(f32)).astype(bf16)

    return local_call(body, [(one.shape, bf16)], one, other)[0]


Z_ORDER = (2, 1, 3, 0)
PIECES = (64, 16, 32, 16, 16, 16, 16, 16, 16, 32, 16)


def opposite_body(p0, one, other, z2a, z2b):
    total = p0[:16].astype(f32) + one[...].astype(f32) + other[...].astype(f32)
    z2a[...] = total[:8].astype(bf16)
    z2b[...] = total[8:].astype(bf16)


def neighbours_body(p0, one, other, from_left, from_right, z1, z3):
    total = p0[16:48].astype(f32) + one[...].astype(f32) + other[...].astype(f32)
    z1[:8] = (total[:8] + from_left[...].astype(f32)).astype(bf16)
    z1[8:] = total[8:16].astype(bf16)
    z3[:8] = total[16:24].astype(bf16)
    z3[8:] = (total[24:] + from_right[...].astype(f32)).astype(bf16)


def scatter_tp(p0, p1z2, p1z13, p1z0, p2z2, p2z1, p2z3, p2z0, p3z2, p3z13, p3z0):
    width = p0.shape[1]
    block, half = ((ROWS, width), bf16), ((ROWS // 2, width), bf16)
    a2 = pp(p2z2, "y", 1)
    a3 = pp(p2z3, "y", -1)
    a1 = pp(p2z1, "y", 1)
    left2 = pp(p3z2, "y", -1)
    a0 = pp(p2z0, "y", -1)
    right2 = pp(add(p1z2, a2, 0), "y", 1)
    right13 = pp(add(p1z13, a1, 0), "y", 1)
    left13 = pp(add(p3z13, a3, 16), "y", -1)
    z2a, z2b = local_call(opposite_body, [half] * 2, p0, right2, left2)
    from_left = pp(z2a, "zh", 1)
    from_right = pp(z2b, "zh", -1)
    right0 = pp(p1z0, "y", 1)
    left0 = pp(add(p3z0, a0, 0), "y", -1)
    z1, z3 = local_call(neighbours_body, [block] * 2, p0, right13, left13, from_left, from_right)
    r1 = pp(z1, "zh", 1)
    r3 = pp(z3, "zh", -1)
    return p0, right0, left0, r1, r3


def update_body(x_ref, p0, right0, left0, r1, r3, x_out):
    total = p0[48:].astype(f32) + right0[...].astype(f32) + left0[...].astype(f32)
    total += r1[...].astype(f32) + r3[...].astype(f32)
    x_out[...] = x_ref[...] + step_size * total


def norm_body(x_ref, gain_ref, h_out):
    x = x_ref[...]
    scale = lax.rsqrt(jnp.mean(x * x, axis=-1, keepdims=True) + eps_norm)
    h_out[...] = (x * scale * gain_ref[...]).astype(bf16)


def exchange_kv(kv):
    other = pp(kv, "zl", 1)
    own_p1 = pp(kv, "x", -1)
    own_m1 = pp(kv, "x", 1)
    other_p1 = pp(other, "x", -1)
    own_m2 = pp(own_m1, "x", 1)
    other_m1 = pp(own_m1, "zl", 1)
    other_p2a = pp(other_p1[:SEG], "x", -1)
    other_p2b = pp(own_m2[SEG:], "zl", 1)
    other_p2 = jnp.concatenate([other_p2a, other_p2b], 0)
    return (kv, other), (own_m1, other_m1, own_p1, other_p1), (own_m2, other_p2)


def group_segments():
    x, zl, c = (lax.axis_index(name) for name in ("x", "zl", "c"))
    ids = []
    for dx in (0, 3, 1, 2):
        for dz in range(2):
            for dc in range(2):
                ids.append((x + dx) % 4 * 4 + (zl + dz) % 2 * 2 + (c + dc) % 2)
    return jnp.stack(ids).astype(jnp.int32)


CHUNKS = 4


def qkv_body(ids_ref, *refs):
    gain_ref, w_ref, kv_ref, q_ref, send_ref, w_here, arrived = refs[13:]
    block = w_ref.shape[1] // CHUNKS

    def copy_of(part, chunk):
        at = (part, pl.ds(pl.multiple_of(chunk * block, block), block), slice(None))
        return pltpu.make_async_copy(w_ref.at[at], w_here.at[at], arrived.at[part * CHUNKS + chunk])

    def dot_of(part, chunk):
        copy_of(part, chunk).wait()
        inner = pl.ds(pl.multiple_of(chunk * block, block), block)
        h = jnp.concatenate([ref[:, inner] for ref in refs[:13]], axis=0)
        return jnp.dot(h, w_here[part, inner, :], preferred_element_type=f32)

    for part in range(3):
        for chunk in range(CHUNKS):
            copy_of(part, chunk).start()
    first = ids_ref[0] % 2 == 0
    for part in range(3):
        product = lax.fori_loop(
            0,
            CHUNKS,
            lambda chunk, total, part=part: total + dot_of(part, chunk),
            jnp.zeros((SEG, 2 * HD), f32),
        )
        heads = []
        for head in range(2):
            value = product[:, head * HD : (head + 1) * HD]
            if part < 2:
                gain = gain_ref[part : part + 1, pl.ds(head * HD, HD)]
                scale = lax.rsqrt(jnp.mean(value * value, axis=-1, keepdims=True) + eps_norm)
                value = value * scale * gain
            heads.append(value)
        own = jnp.where(first, heads[0], heads[1]).astype(bf16)
        other = jnp.where(first, heads[1], heads[0]).astype(bf16)
        at = (2, 0, 1)[part]
        send_ref[:, pl.ds(at * HD, HD)] = other
        if part == 0:
            q_ref[...] = own
        else:
            kv_ref[:, pl.ds(at * HD, HD)] = own


def attend_group(first, ids_ref, len_ref, pos_ref, queries, pieces, top, acc):
    pos = pos_ref[...]
    ones = jnp.ones((4 * SEG, HD), bf16)
    keys = jnp.concatenate([piece[:, :HD] for piece in pieces], axis=0)
    values = jnp.concatenate([piece[:, HD:] for piece in pieces], axis=0)
    extended = jnp.concatenate([values, ones], axis=1)
    for half in range(2):
        valid = []
        for number in range(4):
            segment = ids_ref[4 * first + number]
            limit = jnp.where(segment <= ids_ref[half], len_ref[segment], 0)
            valid.append(pos < limit)
        valid = jnp.concatenate(valid, axis=1)
        scores = lax.dot_general(
            queries[half], keys, (((1,), (1,)), ((), ())), preferred_element_type=f32
        )
        scores = jnp.where(valid, scores * SCORE_SCALE, -1e30)
        best = jnp.max(scores, axis=-1, keepdims=True)
        if first > 0:
            before = top[half][:, :1]
            best = jnp.maximum(best, before)
            factor = jnp.exp2(before - best)
        weights = jnp.exp2(scores - best).astype(bf16)
        update = jnp.dot(weights, extended, preferred_element_type=f32)
        if first > 0:
            update = acc[half] * factor + update
        acc[half] = update
        top[half] = jnp.broadcast_to(best, (SEG, HD))


def queries_of(q_ref, got_ref):
    return q_ref[...], got_ref[:, pl.ds(2 * HD, HD)]


def attend_own_body(ids_ref, len_ref, pos_ref, q_ref, got_ref, *refs):
    queries = queries_of(q_ref, got_ref)
    attend_group(0, ids_ref, len_ref, pos_ref, queries, refs[:2], *refs[2:])


def attend_near_body(ids_ref, len_ref, pos_ref, q_ref, got_ref, *refs):
    pieces, (top_in, acc_in, w_ref, top, acc, w_out, arrived) = refs[:4], refs[4:]
    copies = []
    rows = w_ref.shape[0] // CHUNKS
    for chunk in range(CHUNKS):
        at = (pl.ds(chunk * rows, rows), slice(None))
        copies.append(pltpu.make_async_copy(w_ref.at[at], w_out.at[at], arrived.at[chunk]))
    for copy in copies:
        copy.start()
    top[...] = top_in[...]
    acc[...] = acc_in[...]
    for first in (1, 2):

        @pl.when(ids_ref[4 * first] < ids_ref[0])
        def _(first=first):
            queries = queries_of(q_ref, got_ref)
            group = pieces[2 * first - 2 : 2 * first]
            attend_group(first, ids_ref, len_ref, pos_ref, queries, group, top, acc)

    for copy in copies:
        copy.wait()


def attend_far_body(ids_ref, len_ref, pos_ref, q_ref, got_ref, *refs):
    pieces, (top_in, acc_in), outs, (top, acc) = refs[:2], refs[2:4], refs[4:6], refs[6:]
    top[...] = top_in[...]
    acc[...] = acc_in[...]

    @pl.when(ids_ref[12] < ids_ref[0])
    def _():
        queries = queries_of(q_ref, got_ref)
        attend_group(3, ids_ref, len_ref, pos_ref, queries, pieces, top, acc)

    for half, out in enumerate(outs):
        out[...] = (acc[half, :, :HD] / acc[half, :, HD:]).astype(bf16)


def project_body(ids_ref, own_ref, other_ref, w_ref, *outs):
    own, other = own_ref[...], other_ref[...]
    first = ids_ref[0] % 2 == 0
    attended = jnp.where(
        first, jnp.concatenate([own, other], axis=1), jnp.concatenate([other, own], axis=1)
    )
    order = [4 * y + G_ORDER.index(z) for y in range(4) for z in Z_ORDER]
    attended = jnp.concatenate([attended[16 * at : 16 * at + 16] for at in order], axis=0)
    block = 1024
    for at in range(0, w_ref.shape[1], block):
        cols = pl.ds(at, block)
        partial = jnp.dot(attended, w_ref[:, cols], preferred_element_type=f32).astype(bf16)
        row = 0
        for out in outs:
            out[:, cols] = partial[row : row + out.shape[0]]
            row += out.shape[0]


def shards(states, norm_gain, qkv_weight, qk_gain, out_weight, segment_lengths):
    w = jnp.transpose(qkv_weight, (1, 0, 2))
    width = states.shape[1]
    y, zh = lax.axis_index("y"), lax.axis_index("zh")
    row = jnp.arange(SEG, dtype=jnp.int32)
    at = row // 16 % 4
    z_block = sum(jnp.where(at == place, block, 0) for place, block in enumerate(G_ORDER))
    device = (y + row // 64) % 4 * 4 + (zh + z_block) % 4
    pos = (device * ROWS + row % ROWS)[None, :]
    ids = group_segments()
    state = [((2, SEG, HD), f32), ((2, SEG, 2 * HD), f32)]
    scratch = [pltpu.VMEM(shape, dtype) for shape, dtype in state]
    partials = [((rows, width), bf16) for rows in PIECES]
    landed = pltpu.SemaphoreType.DMA((CHUNKS,))
    w_scratch = [pltpu.VMEM(w.shape, bf16), pltpu.SemaphoreType.DMA((3 * CHUNKS,))]
    projected = [((SEG, cols * HD), bf16) for cols in (2, 1, 3)]
    columns = [((SEG, HD), bf16)] * 2

    def one_step(step_index, current):
        h = local_call(norm_body, [((ROWS, width), bf16)], current, norm_gain[None, :])[0]
        operands = (ids, *gather_tp(h), qk_gain, w)
        kv, q, send = local_call(qkv_body, projected, *operands, scratch=w_scratch, in_hbm=1)
        got = pp(send, "c", 1)
        own, near, far = exchange_kv(jnp.concatenate([kv, got[:, : 2 * HD]], 0))
        common = (ids, segment_lengths, pos, q, got)
        running = local_call(attend_own_body, state, *common, *own)
        *running, w_out = local_call(
            attend_near_body,
            state + [(out_weight.shape, bf16)],
            *common,
            *near,
            *running,
            out_weight,
            scratch=[landed],
            in_hbm=1,
        )
        mine, others = local_call(
            attend_far_body, columns, *common, *far, *running, scratch=scratch
        )
        operands = (ids, mine, pp(others, "c", 1), w_out)
        moved = scatter_tp(*local_call(project_body, partials, *operands))
        return local_call(update_body, [((ROWS, width), f32)], current, *moved)[0]

    return lax.fori_loop(0, STEPS, one_step, states)


def solution(mesh):
    inner = Mesh(mesh.devices.reshape(4, 2, 2, 4, 4), ("x", "zl", "c", "y", "zh"))
    tm, tp = ("x", "zl", "c"), ("y", "zh")
    return jax.shard_map(
        shards,
        mesh=inner,
        in_specs=(P(tm + tp, None), P(), P(None, None, tp), P(None, tp), P(tp, None), P()),
        out_specs=P(tm + tp, None),
        check_vma=False,
    )
```

```python
import jax
import jax.numpy as jnp
from jax import lax
from jax.experimental import pallas as pl
from jax.experimental.pallas import tpu as pltpu
from jax.sharding import Mesh, PartitionSpec as P


HD = 128
STEPS = 2
SEG = 256
ROWS = 16
eps_norm = 1e-06
step_size = -0.5
f32 = jnp.float32
bf16 = jnp.bfloat16
SCORE_SCALE = 1.4426950408889634 * HD ** (-0.5)


def pp(value, axis, steps):
    count = lax.axis_size(axis)
    return lax.ppermute(value, axis, [(i, (i + steps) % count) for i in range(count)])


G_ORDER = (0, 1, 3, 2)


def gather_tp(h):
    half = ROWS // 2
    b1 = pp(h, "zh", -1)
    b3 = pp(h, "zh", 1)
    own_p1 = pp(h, "y", -1)
    own_m1 = pp(h, "y", 1)
    b2_a = pp(b3[:half], "zh", 1)
    b2_b = pp(b1[half:], "zh", -1)
    own_m2 = pp(own_m1, "y", 1)
    mid = jnp.concatenate([b1, b3], 0)
    mid_p1 = pp(mid, "y", -1)
    mid_m1 = pp(mid, "y", 1)
    last = jnp.concatenate([b2_a, b2_b], 0)
    last_p1 = pp(last, "y", -1)
    last_m1 = pp(last, "y", 1)
    mid_p2 = pp(mid_p1[ROWS:], "y", -1)
    mid_m2 = pp(mid_m1[:ROWS], "y", 1)
    last_p2 = pp(last_p1, "y", -1)
    near = (h, mid, last, own_p1, mid_p1, last_p1)
    return near + (own_m2, mid_m2, mid_p2, last_p2, own_m1, mid_m1, last_m1)


def local_call(body, out, *operands, scratch=(), in_hbm=0):
    vmem = pl.BlockSpec(memory_space=pltpu.VMEM)
    smem = pl.BlockSpec(memory_space=pltpu.SMEM)
    anywhere = pl.BlockSpec(memory_space=pl.ANY)
    specs, values = [], []
    for number, value in enumerate(operands):
        if number >= len(operands) - in_hbm:
            specs.append(anywhere)
            value = pltpu.with_memory_space_constraint(value, pltpu.HBM)
        elif value.ndim == 1:
            specs.append(smem)
        else:
            specs.append(vmem)
            value = pltpu.with_memory_space_constraint(value, pltpu.VMEM)
        values.append(value)
    return pl.pallas_call(
        body,
        in_specs=specs,
        out_specs=[vmem] * len(out),
        out_shape=[pltpu.VMEM(shape, dtype) for shape, dtype in out],
        scratch_shapes=scratch,
        compiler_params=pltpu.CompilerParams(vmem_limit_bytes=24 << 20),
    )(*values)


def prefetch(source, after, part):
    def body(after_ref, source_ref, out_ref, arrived):
        del after_ref
        copy = pltpu.make_async_copy(source_ref.at[part], out_ref, arrived)
        copy.start()
        copy.wait()

    anywhere = pl.BlockSpec(memory_space=pl.ANY)
    return pl.pallas_call(
        body,
        in_specs=[anywhere, anywhere],
        out_specs=pl.BlockSpec(memory_space=pltpu.VMEM),
        out_shape=pltpu.VMEM(source.shape[1:], source.dtype),
        scratch_shapes=[pltpu.SemaphoreType.DMA],
        compiler_params=pltpu.CompilerParams(vmem_limit_bytes=1 << 20),
        name="prefetch",
    )(after, pltpu.with_memory_space_constraint(source, pltpu.HBM))


def add(one, other, at):
    def body(one_ref, other_ref, out_ref):
        window = pl.ds(at, other.shape[0])
        if other.shape != one.shape:
            out_ref[...] = one_ref[...]
        out_ref[window, :] = (one_ref[window, :].astype(f32) + other_ref[...].astype(f32)).astype(bf16)

    return local_call(body, [(one.shape, bf16)], one, other)[0]


Z_ORDER = (2, 1, 3, 0)
PIECES = (64, 16, 32, 16, 16, 16, 16, 16, 16, 32, 16)


def opposite_body(p0, one, other, z2a, z2b):
    total = p0[:16].astype(f32) + one[...].astype(f32) + other[...].astype(f32)
    z2a[...] = total[:8].astype(bf16)
    z2b[...] = total[8:].astype(bf16)


def neighbours_body(p0, one, other, from_left, from_right, z1, z3):
    total = p0[16:48].astype(f32) + one[...].astype(f32) + other[...].astype(f32)
    z1[:8] = (total[:8] + from_left[...].astype(f32)).astype(bf16)
    z1[8:] = total[8:16].astype(bf16)
    z3[:8] = total[16:24].astype(bf16)
    z3[8:] = (total[24:] + from_right[...].astype(f32)).astype(bf16)


def scatter_tp(p0, p1z2, p1z13, p1z0, p2z2, p2z1, p2z3, p2z0, p3z2, p3z13, p3z0):
    width = p0.shape[1]
    block, half = ((ROWS, width), bf16), ((ROWS // 2, width), bf16)
    a2 = pp(p2z2, "y", 1)
    a3 = pp(p2z3, "y", -1)
    a1 = pp(p2z1, "y", 1)
    left2 = pp(p3z2, "y", -1)
    a0 = pp(p2z0, "y", -1)
    right2 = pp(add(p1z2, a2, 0), "y", 1)
    right13 = pp(add(p1z13, a1, 0), "y", 1)
    left13 = pp(add(p3z13, a3, 16), "y", -1)
    z2a, z2b = local_call(opposite_body, [half] * 2, p0, right2, left2)
    from_left = pp(z2a, "zh", 1)
    from_right = pp(z2b, "zh", -1)
    right0 = pp(p1z0, "y", 1)
    left0 = pp(add(p3z0, a0, 0), "y", -1)
    z1, z3 = local_call(neighbours_body, [block] * 2, p0, right13, left13, from_left, from_right)
    r1 = pp(z1, "zh", 1)
    r3 = pp(z3, "zh", -1)
    return p0, right0, left0, r1, r3


def normed(x, gain_ref):
    scale = lax.rsqrt(jnp.mean(x * x, axis=-1, keepdims=True) + eps_norm)
    return (x * scale * gain_ref[...]).astype(bf16)


def norm_body(x_ref, gain_ref, h_out):
    h_out[...] = normed(x_ref[...], gain_ref)


def update_body(x_ref, gain_ref, p0, right0, left0, r1, r3, x_out, h_out):
    total = p0[48:].astype(f32) + right0[...].astype(f32) + left0[...].astype(f32)
    total += r1[...].astype(f32) + r3[...].astype(f32)
    x = x_ref[...] + step_size * total
    x_out[...] = x
    h_out[...] = normed(x, gain_ref)


def exchange_kv(kv):
    other = pp(kv, "zl", 1)
    own_p1 = pp(kv, "x", -1)
    own_m1 = pp(kv, "x", 1)
    other_p1 = pp(other, "x", -1)
    own_m2 = pp(own_m1, "x", 1)
    other_m1 = pp(own_m1, "zl", 1)
    other_p2a = pp(other_p1[:SEG], "x", -1)
    other_p2b = pp(own_m2[SEG:], "zl", 1)
    other_p2 = jnp.concatenate([other_p2a, other_p2b], 0)
    return (kv, other), (own_m1, other_m1), (own_p1, other_p1), (own_m2, other_p2)


def group_segments():
    x, zl, c = (lax.axis_index(name) for name in ("x", "zl", "c"))
    ids = []
    for dx in (0, 3, 1, 2):
        for dz in range(2):
            for dc in range(2):
                ids.append((x + dx) % 4 * 4 + (zl + dz) % 2 * 2 + (c + dc) % 2)
    return jnp.stack(ids).astype(jnp.int32)


CHUNKS = 4


def qkv_body(ids_ref, *refs):
    gain_ref, *w_refs, kv_ref, q_ref, send_ref = refs[13:]
    block = w_refs[0].shape[0] // 2

    def dot_of(w_ref, chunk):
        inner = pl.ds(pl.multiple_of(chunk * block, block), block)
        h = jnp.concatenate([ref[:, inner] for ref in refs[:13]], axis=0)
        return jnp.dot(h, w_ref[inner, :], preferred_element_type=f32)

    first = ids_ref[0] % 2 == 0
    for part in range(3):
        product = lax.fori_loop(
            0,
            2,
            lambda chunk, total, part=part: total + dot_of(w_refs[part], chunk),
            jnp.zeros((SEG, 2 * HD), f32),
        )
        heads = []
        for head in range(2):
            value = product[:, head * HD : (head + 1) * HD]
            if part < 2:
                gain = gain_ref[part : part + 1, pl.ds(head * HD, HD)]
                scale = lax.rsqrt(jnp.mean(value * value, axis=-1, keepdims=True) + eps_norm)
                value = value * scale * gain
            heads.append(value)
        own = jnp.where(first, heads[0], heads[1]).astype(bf16)
        other = jnp.where(first, heads[1], heads[0]).astype(bf16)
        at = (2, 0, 1)[part]
        send_ref[:, pl.ds(at * HD, HD)] = other
        if part == 0:
            q_ref[...] = own
        else:
            kv_ref[:, pl.ds(at * HD, HD)] = own


def attend_group(first, ids_ref, len_ref, pos_ref, queries, pieces, top, acc):
    pos = pos_ref[...]
    ones = jnp.ones((4 * SEG, HD), bf16)
    keys = jnp.concatenate([piece[:, :HD] for piece in pieces], axis=0)
    values = jnp.concatenate([piece[:, HD:] for piece in pieces], axis=0)
    extended = jnp.concatenate([values, ones], axis=1)
    for half in range(2):
        valid = []
        for number in range(4):
            segment = ids_ref[4 * first + number]
            limit = jnp.where(segment <= ids_ref[half], len_ref[segment], 0)
            valid.append(pos < limit)
        valid = jnp.concatenate(valid, axis=1)
        scores = lax.dot_general(
            queries[half], keys, (((1,), (1,)), ((), ())), preferred_element_type=f32
        )
        scores = jnp.where(valid, scores * SCORE_SCALE, -1e30)
        best = jnp.max(scores, axis=-1, keepdims=True)
        if first > 0:
            before = top[half][:, :1]
            best = jnp.maximum(best, before)
            factor = jnp.exp2(before - best)
        weights = jnp.exp2(scores - best).astype(bf16)
        update = jnp.dot(weights, extended, preferred_element_type=f32)
        if first > 0:
            update = acc[half] * factor + update
        acc[half] = update
        top[half] = jnp.broadcast_to(best, (SEG, HD))


def queries_of(q_ref, got_ref):
    return q_ref[...], got_ref[:, pl.ds(2 * HD, HD)]


def attend_own_body(ids_ref, len_ref, pos_ref, q_ref, got_ref, *refs):
    pieces, (gain_ref, w_ref, top, acc, gain_out, w_out, arrived) = refs[:2], refs[2:]
    copies = [pltpu.make_async_copy(gain_ref, gain_out, arrived.at[CHUNKS])]
    rows = w_ref.shape[0] // CHUNKS
    for chunk in range(CHUNKS):
        at = (pl.ds(chunk * rows, rows), slice(None))
        copies.append(pltpu.make_async_copy(w_ref.at[at], w_out.at[at], arrived.at[chunk]))
    for copy in copies:
        copy.start()
    attend_group(0, ids_ref, len_ref, pos_ref, queries_of(q_ref, got_ref), pieces, top, acc)
    for copy in copies:
        copy.wait()


def attend_one(first):
    def body(ids_ref, len_ref, pos_ref, q_ref, got_ref, *refs):
        pieces, (top_in, acc_in, top, acc) = refs[:2], refs[2:]
        top[...] = top_in[...]
        acc[...] = acc_in[...]

        @pl.when(ids_ref[4 * first] < ids_ref[0])
        def _():
            queries = queries_of(q_ref, got_ref)
            attend_group(first, ids_ref, len_ref, pos_ref, queries, pieces, top, acc)

    return body


def attend_far_body(ids_ref, len_ref, pos_ref, q_ref, got_ref, *refs):
    pieces, (top_in, acc_in), outs, (top, acc) = refs[:2], refs[2:4], refs[4:6], refs[6:]
    top[...] = top_in[...]
    acc[...] = acc_in[...]

    @pl.when(ids_ref[12] < ids_ref[0])
    def _():
        queries = queries_of(q_ref, got_ref)
        attend_group(3, ids_ref, len_ref, pos_ref, queries, pieces, top, acc)

    for half, out in enumerate(outs):
        out[...] = (acc[half, :, :HD] / acc[half, :, HD:]).astype(bf16)


def project_body(ids_ref, own_ref, other_ref, w_ref, *outs):
    own, other = own_ref[...], other_ref[...]
    first = ids_ref[0] % 2 == 0
    attended = jnp.where(
        first, jnp.concatenate([own, other], axis=1), jnp.concatenate([other, own], axis=1)
    )
    order = [4 * y + G_ORDER.index(z) for y in range(4) for z in Z_ORDER]
    attended = jnp.concatenate([attended[16 * at : 16 * at + 16] for at in order], axis=0)
    block = 1024
    for at in range(0, w_ref.shape[1], block):
        cols = pl.ds(at, block)
        partial = jnp.dot(attended, w_ref[:, cols], preferred_element_type=f32).astype(bf16)
        row = 0
        for out in outs:
            out[:, cols] = partial[row : row + out.shape[0]]
            row += out.shape[0]


def shards(states, norm_gain, qkv_weight, qk_gain, out_weight, segment_lengths):
    w = jnp.transpose(qkv_weight, (1, 0, 2))
    width = states.shape[1]
    y, zh = lax.axis_index("y"), lax.axis_index("zh")
    row = jnp.arange(SEG, dtype=jnp.int32)
    at = row // 16 % 4
    z_block = sum(jnp.where(at == place, block, 0) for place, block in enumerate(G_ORDER))
    device = (y + row // 64) % 4 * 4 + (zh + z_block) % 4
    pos = (device * ROWS + row % ROWS)[None, :]
    ids = group_segments()
    state = [((2, SEG, HD), f32), ((2, SEG, 2 * HD), f32)]
    scratch = [pltpu.VMEM(shape, dtype) for shape, dtype in state]
    partials = [((rows, width), bf16) for rows in PIECES]
    landed = pltpu.SemaphoreType.DMA((CHUNKS + 1,))
    projected = [((SEG, cols * HD), bf16) for cols in (2, 1, 3)]
    columns = [((SEG, HD), bf16)] * 2

    gain = norm_gain[None, :]
    rows = [((ROWS, width), f32), ((ROWS, width), bf16)]

    def one_step(step_index, carried):
        current, h = carried
        weights = [prefetch(w, h, part) for part in range(3)]
        operands = (ids, *gather_tp(h), qk_gain, *weights)
        kv, q, send = local_call(qkv_body, projected, *operands)
        got = pp(send, "c", 1)
        own, minus, plus, far = exchange_kv(jnp.concatenate([kv, got[:, : 2 * HD]], 0))
        common = (ids, segment_lengths, pos, q, got)
        *running, gain_here, w_out = local_call(
            attend_own_body,
            state + [(gain.shape, f32), (out_weight.shape, bf16)],
            *common,
            *own,
            gain,
            out_weight,
            scratch=[landed],
            in_hbm=2,
        )
        running = local_call(attend_one(2), state, *common, *plus, *running)
        running = local_call(attend_one(1), state, *common, *minus, *running)
        mine, others = local_call(
            attend_far_body, columns, *common, *far, *running, scratch=scratch
        )
        operands = (ids, mine, pp(others, "c", 1), w_out)
        moved = scatter_tp(*local_call(project_body, partials, *operands))
        return tuple(local_call(update_body, rows, current, gain_here, *moved))

    first = local_call(norm_body, rows[1:], states, gain)[0]
    return lax.fori_loop(0, STEPS, one_step, (states, first))[0]


def solution(mesh):
    inner = Mesh(mesh.devices.reshape(4, 2, 2, 4, 4), ("x", "zl", "c", "y", "zh"))
    tm, tp = ("x", "zl", "c"), ("y", "zh")
    return jax.shard_map(
        shards,
        mesh=inner,
        in_specs=(P(tm + tp, None), P(), P(None, None, tp), P(None, tp), P(tp, None), P()),
        out_specs=P(tm + tp, None),
        check_vma=False,
    )
```
